32 devices in a mesh: groups: 2 (over x), pos: 16 (over z, y, core).
Axes of the slice: x: 2, y: 2, z: 4, core: 2. Of those that a mesh axis runs over, the one named last changes fastest.
Arguments:
- activations: bfloat16 [32768, 512], P(('groups', 'pos')), parts along dimension 0, may hold values from -6 to 6
- kernel: bfloat16 [512, 5, 608], P('pos'), may hold values from -0.125 to 0.125
- cotangent: bfloat16 [16384, 608], P(('groups', 'pos')), parts along dimension 0, may hold values from -6 to 6
Outputs:
- pooled: bfloat16 [16384, 608], P(('groups', 'pos')), parts along dimension 0
- input_grad: bfloat16 [32768, 512], P(('groups', 'pos')), parts along dimension 0
- kernel_grad: float32 [1024, 5, 608], P(('groups', 'pos')), parts along dimension 0
The draws below stay inside these ranges and needn't reach their ends.
There are 2 independent parts, one for each index of `groups`. The reference program is written for one: setup_inputs(seed, part) draws one part's arguments, and reference() takes and returns one part's arrays. A program takes and returns all parts, laid end to end along the dimension named above; an argument that names none is the same for every part. Nothing has to cross between parts.
All inputs are finite; a program needn't handle non-finite values.
Results may differ from the reference program's by a relative error of at most 0.0041.
Values may be sent and summed in bfloat16 or wider, within the bound.
A program may use at most 128 MiB of HBM per device.

```python
import jax
import jax.numpy as jnp

CIN = 512
COUT = 608
KERNEL_TAPS = 5
DILATION_STEP = 4
TOKENS = 16384


def strengthened(drawn, own_key, source, target, parts, factor):
    def block_of(position):
        return (jnp.arange(drawn.shape[position]) // (drawn.shape[position] // parts)).reshape((-1,) + (1,) * (drawn.ndim - 1 - position))

    first = jax.random.permutation(own_key, parts)[block_of(target)]
    other_side = (block_of(target) + parts // 2) % parts
    return jnp.where((block_of(source) == first) | (block_of(source) == other_side), factor * drawn, drawn)


def steps_of(own_key, dims, pieces, smallest, high):
    def one(axis_at, blocks):
        steps = jax.random.uniform(jax.random.fold_in(jax.random.fold_in(own_key, 6), axis_at), (blocks,), jnp.float32, smallest / len(pieces), high / len(pieces))
        return jnp.repeat(jnp.exp(steps), dims[axis_at] // blocks).reshape((-1,) + (1,) * (len(dims) - axis_at - 1))

    loudness = one(*pieces[0])
    for cut in pieces[1:]:
        loudness = loudness * one(*cut)
    return loudness


def centred(stream_key, shape, deviation, reach, pieces=(), held_as=jnp.bfloat16):
    loudness = steps_of(stream_key, shape, pieces, -0.22, 0.18) if pieces else 1.0
    entries = jax.random.normal(stream_key, shape, jnp.float32) * deviation * loudness
    return jnp.minimum(jnp.maximum(entries, -reach), reach).astype(held_as)


def bell_draw_with(rng, extent, width, limit, shards, heavy, held_as=jnp.bfloat16):
    entries = width * jax.random.normal(rng, extent, jnp.float32)
    if shards:
        entries = entries * steps_of(rng, extent, shards, -0.22, 0.18)
    return jnp.clip(strengthened(entries, jax.random.fold_in(rng, 3), *heavy), -limit, limit).astype(held_as)


def setup_inputs(seed: int = 0, part: int = 0) -> dict:
    key_of = jax.random.split(jax.random.key(seed), 4)
    part_keys = jax.random.split(jax.random.fold_in(key_of[3], part), 4)
    return {
        "activations": bell_draw_with(part_keys[0], (TOKENS, CIN), 1.0, 6.0, ((0, 16),), (0, 1, 16, 2.0)),
        "kernel": centred(key_of[1], (CIN, KERNEL_TAPS, COUT), (CIN * KERNEL_TAPS) ** -0.5, 0.125, ((0, 16),)),
        "cotangent": centred(part_keys[2], (TOKENS // 2, COUT), 1.0, 6.0, ((0, 16),)),
    }


def gelu_value(v):
    return 0.5 * v * (1.0 + jax.scipy.special.erf(v * 0.7071067811865476))


def gelu_slope(v):
    return 0.5 * (1.0 + jax.scipy.special.erf(v * 0.7071067811865476)) + v * jnp.exp(-0.5 * v * v) * 0.3989422804014327


def reference(activations, kernel, cotangent):
    window_length = activations.shape[0]
    reach_row_count = (KERNEL_TAPS - 1) // 2 * DILATION_STEP
    values = activations.astype(jnp.float32)
    gelu = gelu_value(values).astype(jnp.bfloat16)
    padded_activation = jnp.pad(gelu, ((reach_row_count, reach_row_count), (0, 0)))
    dilated_output = jnp.zeros((window_length, kernel.shape[2]), jnp.float32)
    for tap_offset in range(KERNEL_TAPS):
        dilated_output = dilated_output + jnp.dot(padded_activation[tap_offset * DILATION_STEP:tap_offset * DILATION_STEP + window_length], kernel[:, tap_offset, :], preferred_element_type=jnp.float32)
    pooled = (0.5 * dilated_output.reshape(window_length // 2, 2, -1).sum(axis=1)).astype(jnp.bfloat16)
    convolution_gradient = (0.5 * jnp.repeat(cotangent.astype(jnp.float32), 2, axis=0)).astype(jnp.bfloat16)
    gradient_pieces = []
    for tap_offset in range(KERNEL_TAPS):
        gradient_pieces.append(jnp.dot(padded_activation[tap_offset * DILATION_STEP:tap_offset * DILATION_STEP + window_length].T, convolution_gradient, preferred_element_type=jnp.float32))
    kernel_grad = jnp.stack(gradient_pieces, axis=1)
    padded_gradient = jnp.pad(convolution_gradient, ((reach_row_count, reach_row_count), (0, 0)))
    gelu_grad = jnp.zeros((window_length, kernel.shape[0]), jnp.float32)
    for tap_offset in range(KERNEL_TAPS):
        leading_rows = (KERNEL_TAPS - 1 - tap_offset) * DILATION_STEP
        gelu_grad = gelu_grad + jnp.dot(padded_gradient[leading_rows:leading_rows + window_length], kernel[:, tap_offset, :].T, preferred_element_type=jnp.float32)
    input_grad = (gelu_grad * gelu_slope(values)).astype(jnp.bfloat16)
    return pooled, input_grad, kernel_grad
```

```python
import functools

import jax
import jax.numpy as jnp
from jax import lax
from jax.experimental import pallas as pl
from jax.experimental.pallas import tpu as pltpu
from jax.sharding import PartitionSpec as P

DILATION_STEP = 4


def extended(cells, sides, width):
    for axis, dim in sides:
        count = lax.axis_size(axis)
        ends = count - 1
        head = lax.slice_in_dim(cells, 0, width, axis=dim)
        tail = lax.slice_in_dim(cells, cells.shape[dim] - width, cells.shape[dim], axis=dim)
        cells = jnp.concatenate(
            [
                lax.ppermute(tail, axis, [(i, (i + 1) % count) for i in range(ends)]),
                cells,
                lax.ppermute(head, axis, [((i + 1) % count, i) for i in range(ends)]),
            ],
            axis=dim,
        )
    return cells


def gelu_value(v):
    return 0.5 * v * (1.0 + jax.scipy.special.erf(v * 0.7071067811865476))


def gelu_slope(v):
    return (
        0.5 * (1.0 + jax.scipy.special.erf(v * 0.7071067811865476))
        + v * jnp.exp(-0.5 * v * v) * 0.3989422804014327
    )


def on_device(activations, kernel, cotangent):
    window_length = activations.shape[0]
    kernel_taps = kernel.shape[1]
    out_width = kernel.shape[2]
    reach_row_count = (kernel_taps - 1) // 2 * DILATION_STEP
    values = activations.astype(jnp.float32)
    gelu = gelu_value(values).astype(jnp.bfloat16)
    padded_activation = extended(gelu, (("pos", 0),), reach_row_count)
    gelu_taps = jnp.stack(
        [
            padded_activation[
                tap_offset * DILATION_STEP : tap_offset * DILATION_STEP + window_length
            ]
            for tap_offset in range(kernel_taps)
        ]
    )
    kernel_full = lax.all_gather(kernel, "pos", axis=0, tiled=True)
    columns = gelu_taps
    dilated_output = jnp.einsum(
        "kpc,cko->po", columns, kernel_full, preferred_element_type=jnp.float32
    )
    pooled = (0.5 * dilated_output.reshape(window_length // 2, 2, out_width).sum(axis=1)).astype(
        jnp.bfloat16
    )
    convolution_gradient = (0.5 * jnp.repeat(cotangent.astype(jnp.float32), 2, axis=0)).astype(
        jnp.bfloat16
    )
    columns = gelu_taps
    kernel_grad = lax.psum_scatter(
        jnp.einsum(
            "kpc,po->cko", columns, convolution_gradient, preferred_element_type=jnp.float32
        ),
        "pos",
        scatter_dimension=0,
        tiled=True,
    )
    padded_gradient = extended(convolution_gradient, (("pos", 0),), reach_row_count)
    grad_taps = jnp.stack(
        [
            padded_gradient[
                (kernel_taps - 1 - tap_offset)
                * DILATION_STEP : (kernel_taps - 1 - tap_offset)
                * DILATION_STEP
                + window_length
            ]
            for tap_offset in range(kernel_taps)
        ]
    )
    block = jnp.einsum("kpo,cko->pc", grad_taps, kernel_full, preferred_element_type=jnp.float32)
    input_grad = (block * gelu_slope(values)).astype(jnp.bfloat16)
    return (pooled, input_grad, kernel_grad)


MESH = pl.DeviceIdType.MESH
F32 = jnp.float32
BF16 = jnp.bfloat16
PAD = 8
EDGE = 16
LANES = 128

WORK = (
    ("start",),
    ("gelu",),
    ("cot",),
    ("slope", 0),
    ("slope", 1),
    ("slope", 2),
    ("halo",),
    ("dot", 0),
    ("dot", 1),
    ("dot", 2),
    ("dot", 3),
    ("slope", 3),
    ("cf", 0),
    ("cb", 0),
    ("ig", 0),
    ("cf", 1),
    ("cb", 1),
    ("ig", 1),
    ("cf", 2),
    ("cb", 2),
    ("ig", 2),
    ("cf", 3),
    ("cb", 3),
    ("ig", 3),
)
END = (
    (),
    (),
    (),
    (),
    (),
    (),
    (),
    (),
    (("tz", 1, 0, 0),),
    (("ty", 0),),
    (("ty", 1), ("tz", 1, 0, 1), ("ys", 0),),
    (("ys", 1), ("ys", 2), ("tz", 1, 1, 0), ("yk", 0), ("yk", 1), ("yk", 2),),
    (("ys", 3), ("tz", 2, 0, 0), ("yk", 3), ("zs", 0, 0), ("tx", 0, 1), ("tz", 1, 1, 1),),
    (("tz", 2, 0, 1), ("tx", 1, 0), ("zs", 0, 1),),
    (("tz", 3, 0, 0), ("zs", 0, 2), ("tz", 2, 1, 0),),
    (("zs", 1, 0), ("tx", 1, 1), ("tz", 2, 1, 1),),
    (("tz", 3, 0, 1), ("tx", 2, 0), ("zs", 1, 1),),
    (("tz", 3, 1, 0), ("zs", 1, 2),),
    (("tz", 3, 1, 1), ("zs", 2, 0), ("tx", 2, 1),),
    (("tx", 3, 0), ("zs", 2, 1),),
    (("zs", 2, 2),),
    (("tx", 3, 1), ("zs", 3, 0),),
    (),
    (("zs", 3, 1),),
    (("zs", 3, 2),),
)
INNER = (
    (),
    (),
    (),
    (),
    (),
    (),
    (),
    (),
    (("tz", 1, 0, 0), ("ty", 0), ("tz", 2, 0, 0),),
    (),
    (("ty", 1), ("tz", 1, 0, 1), ("tz", 2, 0, 1), ("ys", 0),),
    (("tz", 3, 0, 0), ("ys", 1), ("ys", 2), ("yk", 0), ("tz", 1, 1, 0), ("yk", 1), ("tz", 2, 1, 0), ("yk", 2),),
    (("ys", 3), ("yk", 3), ("tz", 1, 1, 1), ("tz", 2, 1, 1), ("tx", 0, 1), ("tz", 3, 0, 1), ("zs", 0, 0),),
    (("tz", 3, 1, 0), ("tx", 1, 0),),
    (("tz", 3, 1, 1), ("tx", 2, 0),),
    (("zs", 1, 0), ("zs", 0, 1), ("zs", 0, 2), ("tx", 1, 1), ("zs", 2, 0),),
    (("tx", 2, 1), ("zs", 1, 1),),
    (("tx", 3, 0), ("zs", 2, 1),),
    (("zs", 1, 2),),
    (),
    (("tx", 3, 1), ("zs", 2, 2), ("zs", 3, 0),),
    (),
    (("zs", 3, 1),),
    (),
    (("zs", 3, 2),),
)
PIECES = ((0, 2), (2, 3))
GROUPS = ((0, 1), (1, 2), (3, 2))


def step_kernel(
    dims,
    act, kern, cot,
    pooled_t, igrad, kgrad,
    weights, actv, cotv, slope, pairs32, g2x, dx,
    part, send1, recv1, send2, recv2, acc, send3, recv3,
    ahalo, dhalo, spread, psum, spans,
    own_sem, a_sem, c_sem, ah_s, ah_r, dh_s, dh_r,
    az_s, az_r, ay_s, ay_r, ax_s, ax_r, ac_s, ac_r,
    r1_s, r1_r, r2_s, r2_r, r3_s, r3_r,
):
    n, A, taps, rows, T2, cin, cout = dims
    step = DILATION_STEP // 2
    mid = (taps - 1) // 2
    g = lax.axis_index("groups")
    p = lax.axis_index("pos")
    c = p % 2
    y = (p // 2) % 2
    z = p // 4
    high, low = z // 2, z % 2
    inner = jnp.logical_and(z > 0, z < A - 1)

    def copy(src, dst, ssem, rsem, to):
        return pltpu.make_async_remote_copy(
            src_ref=src, dst_ref=dst, send_sem=ssem, recv_sem=rsem, device_id=to, device_id_type=MESH
        )

    def at(zz, yy, cc):
        return (g, zz * 4 + yy * 2 + cc)

    core_peer, y_peer, x_peer = at(z, y, 1 - c), at(z, 1 - y, c), (1 - g, p)
    left, right = (g, (p + n - 1) % n), (g, (p + 1) % n)
    beside = (g, (p + n + 2 * c - 1) % n)

    order = (3 * (1 - high), 2 + high - 2 * low, 1 + low, z)
    near = (z, z + 1 - 2 * low, 2 - high, (A - 1) * (1 - high))
    onward = (None, A - 1 - z, near[1], near[1])

    own = pltpu.make_async_copy(kern, weights.at[:, z, y, c], own_sem)
    acts = [
        pltpu.make_async_copy(act.at[:, pl.ds(j * LANES, LANES)], actv.at[j], a_sem.at[j])
        for j in range(A)
    ]
    cots = pltpu.make_async_copy(cot, cotv, c_sem)
    own.start()
    for one in acts:
        one.start()
    cots.start()

    barrier = pltpu.get_barrier_semaphore()
    for peer in (core_peer, beside, y_peer, x_peer, at(near[1], y, c)):
        pl.semaphore_signal(barrier, inc=1, device_id=peer, device_id_type=MESH)

    @pl.when(inner)
    def _():
        pl.semaphore_signal(barrier, inc=1, device_id=at(near[2], y, c), device_id_type=MESH)
        pl.semaphore_wait(barrier, 6)

    @pl.when(jnp.logical_not(inner))
    def _():
        pl.semaphore_wait(barrier, 5)

    def column(j):
        return (y, 1 - y)[j]

    def share(zz, yy, half, q):
        return weights.at[pl.ds(PIECES[q][0], PIECES[q][1]), zz, yy, c, half]

    def z_share(src, zz, j, slot, q, to):
        yy = column(j)
        return copy(
            src, share(zz, yy, g, q), az_s.at[slot, j, q], az_r.at[zz, yy, q], at(to, y, c)
        )

    def z_own(j, q, is_inner):
        src = share(z, 1 - y, g, q) if j else kern.at[pl.ds(PIECES[q][0], PIECES[q][1]), g]
        sends = [z_share(src, z, j, 0, q, near[1])]
        if is_inner:
            sends.append(z_share(src, z, j, 4, q, near[2]))
        return sends

    def z_onward(i, j, q):
        zz = near[i]
        return z_share(share(zz, column(j), g, q), zz, j, i, q, onward[i])

    def y_share(q):
        return copy(
            kern.at[pl.ds(PIECES[q][0], PIECES[q][1]), g], share(z, y, g, q),
            ay_s.at[q], ay_r.at[q], y_peer,
        )

    def x_share(zz, yy, q):
        block = share(zz, yy, g, q)
        return copy(block, block, ax_s.at[zz, yy, q], ax_r.at[zz, yy, q], x_peer)

    def core_block(zz, yy, src=None):
        block = weights.at[:, zz, yy, c]
        return copy(
            block if src is None else src, block, ac_s.at[zz, yy], ac_r.at[zz, yy], core_peer
        )

    def core_part(s, stage):
        yy = y if stage else 1 - y
        return copy(
            send1.at[s, 1 - c, yy], recv1.at[s, stage],
            r1_s.at[s, stage], r1_r.at[s, stage], core_peer,
        )

    def y_part(s, k):
        piece = pl.ds(GROUPS[k][0], GROUPS[k][1])
        return copy(
            send2.at[s, piece], recv2.at[s, piece], r2_s.at[s, k], r2_r.at[s, k], y_peer
        )

    def z_part(s, k):
        up = (order[s] > z).astype(jnp.int32)
        piece = pl.ds(GROUPS[k][0], GROUPS[k][1])
        return copy(
            send3.at[s, piece], recv3.at[up, order[s], piece],
            r3_s.at[s, k], r3_r.at[up, order[s], k], at(z + 2 * up - 1, y, c),
        )

    def z_arrived(up, d, k):
        got = recv3.at[up, d, pl.ds(GROUPS[k][0], GROUPS[k][1])]
        copy(got, got, r3_s.at[0, k], r3_r.at[up, d, k], y_peer).wait_recv()


    def ty(is_inner, q):
        y_share(q).wait_recv()
        return z_own(1, q, is_inner) + [x_share(z, 1 - y, q)]

    def tz(is_inner, i, j, q):
        zz, yy = near[i], column(j)
        got = share(zz, yy, g, q)
        copy(got, got, az_s.at[i, j, q], az_r.at[zz, yy, q], y_peer).wait_recv()
        return ([z_onward(i, j, q)] if is_inner else []) + [x_share(zz, yy, q)]

    def tx(is_inner, i, j):
        zz, yy = near[i], column(j)
        for q in range(len(PIECES)):
            got = share(zz, yy, 1 - g, q)
            copy(got, got, ax_s.at[zz, yy, q], ax_r.at[zz, yy, q], x_peer).wait_recv()
        return [core_block(zz, yy)]

    def ys(is_inner, s):
        core_part(s, 0).wait_recv()
        sends = []
        for k, (first, count) in enumerate(GROUPS):
            for t in range(first, first + count):
                send2[s, t] = (part[s, t, 1 - y, c] + recv1[s, 0, t].astype(F32)).astype(BF16)
            sends.append(y_part(s, k))
            sends[-1].start()
        return []

    def yk(is_inner, s):
        core_part(s, 1).wait_recv()
        for t in range(taps):
            acc[s, t] = part[s, t, y, c] + recv1[s, 1, t].astype(F32)
        return []

    def zs(is_inner, s, k):
        y_part(s, k).wait_recv()
        d = order[s]
        if s < A - 1:
            ups = [(d > z).astype(jnp.int32)] if is_inner else []
        else:
            ups = [0, 1] if is_inner else [(z > 0).astype(jnp.int32)]
        for up in ups:
            z_arrived(up, d, k)
        for t in range(GROUPS[k][0], GROUPS[k][0] + GROUPS[k][1]):
            total = acc[s, t] + recv2[s, t].astype(F32)
            for up in ups:
                total = total + recv3[up, d, t].astype(F32)
            if s < A - 1:
                send3[s, t] = total.astype(BF16)
            else:
                kgrad[t] = total
        return [z_part(s, k)] if s < A - 1 else []

    handlers = dict(ty=ty, tz=tz, tx=tx, ys=ys, yk=yk, zs=zs)

    def deal_with(i):
        def run(is_inner, events):
            for name, *index in events:
                for one in handlers[name](is_inner, *index):
                    one.start()

        if END[i]:
            pl.when(jnp.logical_not(inner))(lambda: run(False, END[i]))
        if INNER[i]:
            pl.when(inner)(lambda: run(True, INNER[i]))


    al = copy(act.at[pl.ds(0, 16)], ahalo.at[1], ah_s.at[0], ah_r.at[1], left)
    ar = copy(act.at[pl.ds(2 * T2 - 16, 16)], ahalo.at[0], ah_s.at[1], ah_r.at[0], right)
    dl = copy(dx.at[pl.ds(EDGE, 16)], dhalo.at[1], dh_s.at[0], dh_r.at[1], left)
    dr = copy(dx.at[pl.ds(EDGE + T2 - 16, 16)], dhalo.at[0], dh_s.at[1], dh_r.at[0], right)
    keep_left = (p > 0).astype(F32)
    keep_right = (p < n - 1).astype(F32)
    tile = pairs32.shape[0]

    def begin():
        al.start()
        ar.start()

        def first(is_inner):
            for q in range(len(PIECES)):
                y_share(q).start()
                for one in z_own(0, q, is_inner):
                    one.start()

        pl.when(inner)(lambda: first(True))
        pl.when(jnp.logical_not(inner))(lambda: first(False))
        core_block(z, y, kern).start()

    def gelu_of(v):
        e = 0.5 * (1.0 + lax.erf(v * 0.7071067811865476))
        return (v * e).astype(BF16).astype(F32)

    def halved(count):
        return 0.5 * (
            pairs32[pl.ds(0, count, stride=2), :] + pairs32[pl.ds(1, count, stride=2), :]
        )

    def gelu():
        def body(i, carry):
            d = i // (2 * T2 // tile)
            r = i % (2 * T2 // tile)
            at_row = pl.multiple_of(r * tile, tile)
            pairs32[...] = gelu_of(actv[d, pl.ds(at_row, tile), :].astype(F32))
            half = pl.multiple_of(r * (tile // 2), tile // 2)
            g2x[d, pl.ds(PAD + half, tile // 2), :] = halved(tile // 2)
            return carry

        for one in acts:
            one.wait()
        lax.fori_loop(0, A * (2 * T2 // tile), body, 0)

    def cotangent():
        cots.wait()
        for i in range(T2 // LANES):
            dx[pl.ds(EDGE + i * LANES, LANES), :] = cotv[:, pl.ds(i * LANES, LANES)].T
        dl.start()
        dr.start()

    def slopes(d):
        def body(i, carry):
            at_row = pl.multiple_of(i * tile, tile)
            v = actv[d, pl.ds(at_row, tile), :].astype(F32)
            e = 0.25 * (1.0 + lax.erf(v * 0.7071067811865476))
            slope[d, pl.ds(at_row, tile), :] = e + v * jnp.exp(-0.5 * v * v) * 0.19947114020071635
            return carry

        lax.fori_loop(0, 2 * T2 // tile, body, 0)

    def halo():
        al.wait_recv()
        ar.wait_recv()
        for side, keep, at_row in ((0, keep_left, 0), (1, keep_right, PAD + T2)):
            for j in range(A):
                pairs32[pl.ds(0, 16), :] = gelu_of(
                    ahalo[side, :, pl.ds(j * LANES, LANES)].astype(F32)
                )
                g2x[j, pl.ds(at_row, PAD), :] = halved(PAD) * keep

    def dot(s):
        d = order[s]
        left_side = jnp.concatenate(
            [
                g2x[d, pl.ds(PAD + step * (k - mid), T2), :].astype(BF16).T
                for k in range(taps)
            ],
            axis=0,
        )
        term = lax.dot_general(
            left_side, cotv[...], (((1,), (1,)), ((), ())), preferred_element_type=F32
        ).reshape(taps, 2, 2, rows, cout)
        part[s] = term
        for cc in range(2):
            for yy in range(2):
                send1[s, cc, yy] = term[:, yy, cc].astype(BF16)
        core_part(s, 0).start()
        core_part(s, 1).start()

    def conv_weights(i):
        return weights[:, near[i]].reshape(taps * LANES, cout)

    def cf(i):
        zz = near[i]
        if i == 0:
            own.wait()
        for j in range(2):
            got = weights.at[:, zz, column(j), 1 - c]
            copy(
                got, got, ac_s.at[zz, column(j)], ac_r.at[zz, column(j)], core_peer
            ).wait_recv()
        window = jnp.concatenate(
            [
                g2x[zz, pl.ds(PAD + step * (k - mid), T2), :].astype(BF16)
                for k in range(taps)
            ],
            axis=1,
        )
        total = jnp.dot(window, conv_weights(i), preferred_element_type=F32)
        if i > 0:
            total += psum[...]
        if i < A - 1:
            psum[...] = total
        else:
            done = total.astype(BF16)
            for q in range(T2 // LANES):
                pooled_t[:, pl.ds(q * LANES, LANES)] = done[q * LANES : q * LANES + LANES].T

    def cb(i):
        if i == 0:
            dl.wait_recv()
            dr.wait_recv()
            dx[pl.ds(0, EDGE), :] = (dhalo[0].astype(F32) * keep_left).astype(BF16)
            dx[pl.ds(EDGE + T2, EDGE), :] = (dhalo[1].astype(F32) * keep_right).astype(BF16)
        spans[...] = lax.dot_general(
            dx[...], conv_weights(i), (((1,), (1,)), ((), ())), preferred_element_type=F32
        )

    def ig(i):
        grad = spans[pl.ds(EDGE + step * mid, T2), pl.ds(0, LANES)]
        for k in range(1, taps):
            grad += spans[pl.ds(EDGE - step * (k - mid), T2), pl.ds(k * LANES, LANES)]
        spread[pl.ds(0, T2, stride=2), :] = grad
        spread[pl.ds(1, T2, stride=2), :] = grad
        at_lane = pl.multiple_of(near[i] * LANES, LANES)
        igrad[:, pl.ds(at_lane, LANES)] = (spread[...] * slope[near[i]]).astype(BF16)

    work = dict(
        start=begin, gelu=gelu, cot=cotangent, slope=slopes, halo=halo, dot=dot, cf=cf, cb=cb, ig=ig
    )
    for i, (name, *index) in enumerate(WORK):
        deal_with(i)
        work[name](*index)
    deal_with(len(WORK))


    for one in (al, ar, dl, dr):
        one.wait_send()

    def all_sent(is_inner):
        for q in range(len(PIECES)):
            for j in range(2):
                for one in z_own(j, q, is_inner):
                    one.wait_send()
                if is_inner:
                    for i in range(1, A):
                        z_onward(i, j, q).wait_send()

    pl.when(inner)(lambda: all_sent(True))
    pl.when(jnp.logical_not(inner))(lambda: all_sent(False))
    core_block(z, y, kern).wait_send()
    for q in range(len(PIECES)):
        y_share(q).wait_send()
    for i in range(A):
        for j in range(2):
            if i or j:
                for q in range(len(PIECES)):
                    x_share(near[i], column(j), q).wait_send()
                core_block(near[i], column(j)).wait_send()
    for s in range(A):
        core_part(s, 0).wait_send()
        core_part(s, 1).wait_send()
        for k in range(len(GROUPS)):
            y_part(s, k).wait_send()
            if s < A - 1:
                z_part(s, k).wait_send()


def write_out(*refs):
    count = len(refs) // 2
    sems = refs[-1]
    copies = [
        pltpu.make_async_copy(refs[i], refs[count + i], sems.at[i]) for i in range(count)
    ]
    for one in copies:
        one.start()
    for one in copies:
        one.wait()


def on_device_fused(activations, kernel, cotangent):
    n = lax.axis_size("pos")
    A = n // 4
    rows, taps, cout = kernel.shape
    T2 = cotangent.shape[0]
    cin = activations.shape[1]
    dims = (n, A, taps, rows, T2, cin, cout)
    Q, K = len(PIECES), len(GROUPS)
    kern = jnp.transpose(kernel, (1, 0, 2)).reshape(taps, 2, rows // 2, cout)
    vmem = pl.BlockSpec(memory_space=pltpu.VMEM)
    hbm = pl.BlockSpec(memory_space=pltpu.HBM)
    DMA = pltpu.SemaphoreType.DMA
    shapes = (
        jax.ShapeDtypeStruct((cout, T2), BF16),
        jax.ShapeDtypeStruct((2 * T2, cin), BF16),
        jax.ShapeDtypeStruct((taps, rows, cout), F32),
    )
    held = [
        pltpu.with_memory_space_constraint(one, pltpu.HBM)
        for one in (activations, kern, cotangent.T)
    ]
    results = pl.pallas_call(
        functools.partial(step_kernel, dims),
        out_shape=shapes,
        in_specs=[hbm] * 3,
        out_specs=(vmem,) * 3,
        scratch_shapes=[
            pltpu.VMEM((taps, A, 2, 2, 2, rows // 2, cout), BF16),
            pltpu.VMEM((A, 2 * T2, LANES), BF16),
            pltpu.VMEM((cout, T2), BF16),
            pltpu.VMEM((A, 2 * T2, LANES), F32),
            pltpu.VMEM((256, LANES), F32),
            pltpu.VMEM((A, T2 + 2 * PAD, LANES), F32),
            pltpu.VMEM((T2 + 2 * EDGE, cout), BF16),
            pltpu.VMEM((A, taps, 2, 2, rows, cout), F32),
            pltpu.VMEM((A, 2, 2, taps, rows, cout), BF16),
            pltpu.VMEM((A, 2, taps, rows, cout), BF16),
            pltpu.VMEM((A, taps, rows, cout), BF16),
            pltpu.VMEM((A, taps, rows, cout), BF16),
            pltpu.VMEM((A, taps, rows, cout), F32),
            pltpu.VMEM((A - 1, taps, rows, cout), BF16),
            pltpu.VMEM((2, A, taps, rows, cout), BF16),
            pltpu.VMEM((2, 16, cin), BF16),
            pltpu.VMEM((2, 16, cout), BF16),
            pltpu.VMEM((2 * T2, LANES), F32),
            pltpu.VMEM((T2, cout), F32),
            pltpu.VMEM((T2 + 2 * EDGE, taps * LANES), F32),
            DMA, DMA((A,)), DMA, DMA((2,)), DMA((2,)), DMA((2,)), DMA((2,)),
            DMA((A + 1, 2, Q)), DMA((A, 2, Q)), DMA((Q,)), DMA((Q,)),
            DMA((A, 2, Q)), DMA((A, 2, Q)), DMA((A, 2)), DMA((A, 2)),
            DMA((A, 2)), DMA((A, 2)), DMA((A, K)), DMA((A, K)),
            DMA((A, K)), DMA((2, A, K)),
        ],
        compiler_params=pltpu.CompilerParams(
            collective_id=0, has_side_effects=True, vmem_limit_bytes=48 << 20
        ),
    )(*held)
    pooled_t, igrad, kgrad = pl.pallas_call(
        write_out,
        out_shape=shapes,
        in_specs=[vmem] * 3,
        out_specs=(hbm,) * 3,
        scratch_shapes=[DMA((3,))],
        compiler_params=pltpu.CompilerParams(has_side_effects=True, vmem_limit_bytes=1 << 20),
    )(*results)
    return pooled_t.T, igrad, jnp.transpose(kgrad, (1, 0, 2))


def solution(mesh):
    placed = (P(("groups", "pos"), None), P("pos", None, None), P(("groups", "pos"), None))
    n = mesh.shape["pos"]
    fused = n == 16 and mesh.shape["groups"] == 2
    return jax.shard_map(
        on_device_fused if fused else on_device,
        mesh=mesh,
        in_specs=placed,
        out_specs=(
            P(("groups", "pos"), None),
            P(("groups", "pos"), None),
            P(("groups", "pos"), None, None),
        ),
        check_vma=False,
    )
```

```python
import functools

import jax
import jax.numpy as jnp
from jax import lax
from jax.experimental import pallas as pl
from jax.experimental.pallas import tpu as pltpu
from jax.sharding import PartitionSpec as P

DILATION_STEP = 4


def extended(cells, sides, width):
    for axis, dim in sides:
        count = lax.axis_size(axis)
        ends = count - 1
        head = lax.slice_in_dim(cells, 0, width, axis=dim)
        tail = lax.slice_in_dim(cells, cells.shape[dim] - width, cells.shape[dim], axis=dim)
        cells = jnp.concatenate(
            [
                lax.ppermute(tail, axis, [(i, (i + 1) % count) for i in range(ends)]),
                cells,
                lax.ppermute(head, axis, [((i + 1) % count, i) for i in range(ends)]),
            ],
            axis=dim,
        )
    return cells


def gelu_value(v):
    return 0.5 * v * (1.0 + jax.scipy.special.erf(v * 0.7071067811865476))


def gelu_slope(v):
    return (
        0.5 * (1.0 + jax.scipy.special.erf(v * 0.7071067811865476))
        + v * jnp.exp(-0.5 * v * v) * 0.3989422804014327
    )


def on_device(activations, kernel, cotangent):
    window_length = activations.shape[0]
    kernel_taps = kernel.shape[1]
    out_width = kernel.shape[2]
    reach_row_count = (kernel_taps - 1) // 2 * DILATION_STEP
    values = activations.astype(jnp.float32)
    gelu = gelu_value(values).astype(jnp.bfloat16)
    padded_activation = extended(gelu, (("pos", 0),), reach_row_count)
    gelu_taps = jnp.stack(
        [
            padded_activation[
                tap_offset * DILATION_STEP : tap_offset * DILATION_STEP + window_length
            ]
            for tap_offset in range(kernel_taps)
        ]
    )
    kernel_full = lax.all_gather(kernel, "pos", axis=0, tiled=True)
    columns = gelu_taps
    dilated_output = jnp.einsum(
        "kpc,cko->po", columns, kernel_full, preferred_element_type=jnp.float32
    )
    pooled = (0.5 * dilated_output.reshape(window_length // 2, 2, out_width).sum(axis=1)).astype(
        jnp.bfloat16
    )
    convolution_gradient = (0.5 * jnp.repeat(cotangent.astype(jnp.float32), 2, axis=0)).astype(
        jnp.bfloat16
    )
    columns = gelu_taps
    kernel_grad = lax.psum_scatter(
        jnp.einsum(
            "kpc,po->cko", columns, convolution_gradient, preferred_element_type=jnp.float32
        ),
        "pos",
        scatter_dimension=0,
        tiled=True,
    )
    padded_gradient = extended(convolution_gradient, (("pos", 0),), reach_row_count)
    grad_taps = jnp.stack(
        [
            padded_gradient[
                (kernel_taps - 1 - tap_offset)
                * DILATION_STEP : (kernel_taps - 1 - tap_offset)
                * DILATION_STEP
                + window_length
            ]
            for tap_offset in range(kernel_taps)
        ]
    )
    block = jnp.einsum("kpo,cko->pc", grad_taps, kernel_full, preferred_element_type=jnp.float32)
    input_grad = (block * gelu_slope(values)).astype(jnp.bfloat16)
    return (pooled, input_grad, kernel_grad)


MESH = pl.DeviceIdType.MESH
F32 = jnp.float32
BF16 = jnp.bfloat16
PAD = 8
EDGE = 16
LANES = 128

WORK = (
    ("start",),
    ("gelu",),
    ("cot",),
    ("dm",),
    ("slope", 0),
    ("slope", 1),
    ("slope", 2),
    ("slope", 3),
    ("halo",),
    ("dot", 0),
    ("dot", 1),
    ("cf", 0),
    ("cb", 0),
    ("cf", 1),
    ("cb", 1),
    ("cf", 2),
    ("cb", 2),
    ("cv", 3),
)
END = (
    (),
    (),
    (),
    (),
    (),
    (),
    (),
    (),
    (("ty", 0), ("ym", 0), ("tz", 1, 0, 0), ("ym", 1),),
    (),
    (("ty", 1), ("ym", 2), ("ty", 2), ("ym", 3), ("tz", 1, 0, 1),),
    (("ys", 0), ("tz", 1, 0, 2), ("zs", 0, 0), ("tz", 1, 1, 0), ("yk", 0), ("ys", 1), ("tz", 2, 0, 0), ("zs", 1, 0), ("ys", 2), ("zs", 2, 0), ("yk", 1), ("tx", 0, 1), ("tz", 1, 1, 1), ("tz", 1, 1, 2), ("yk", 3), ("yk", 2), ("tz", 2, 0, 1), ("zs", 0, 1), ("tx", 1, 0),),
    (("zs", 0, 2), ("tz", 2, 0, 2), ("tz", 2, 1, 0), ("zs", 0, 3), ("tz", 2, 1, 1),),
    (("zs", 0, 4), ("tx", 1, 1), ("tz", 2, 1, 2), ("zs", 1, 1), ("tz", 3, 0, 0), ("tx", 2, 0), ("ys", 3), ("tz", 3, 0, 1), ("tz", 3, 0, 2), ("zs", 1, 2),),
    (("tz", 3, 1, 0), ("zs", 1, 3), ("tx", 2, 1), ("zs", 1, 4), ("tz", 3, 1, 1), ("tz", 3, 1, 2),),
    (("zs", 2, 1), ("zs", 2, 2),),
    (("tx", 3, 0), ("zs", 2, 3), ("zs", 3, 0),),
    (("tx", 3, 1), ("zs", 2, 4), ("zs", 3, 1), ("zs", 3, 2),),
    (("zs", 3, 3), ("zs", 3, 4),),
)
INNER = (
    (),
    (),
    (),
    (),
    (),
    (),
    (),
    (("ym", 0), ("ym", 1), ("ty", 0),),
    (("tz", 2, 0, 0), ("ym", 2), ("tz", 1, 0, 0), ("ym", 3),),
    (),
    (("ty", 1), ("ty", 2), ("tz", 1, 0, 1), ("tz", 2, 0, 1),),
    (("ys", 0), ("tz", 1, 0, 2), ("tz", 2, 0, 2), ("tz", 2, 1, 0), ("tz", 1, 1, 0), ("tz", 1, 1, 1), ("tz", 1, 1, 2), ("tz", 2, 1, 1), ("ys", 1), ("tx", 0, 1), ("yk", 2), ("tz", 2, 1, 2), ("tz", 3, 0, 0), ("ys", 2), ("zs", 0, 0), ("tz", 3, 0, 1), ("tz", 3, 0, 2), ("yk", 0), ("ys", 3),),
    (("tz", 3, 1, 0), ("zs", 2, 0), ("tz", 3, 1, 1), ("tx", 1, 0), ("tz", 3, 1, 2),),
    (("zs", 0, 1), ("yk", 1), ("zs", 1, 0), ("tx", 1, 1), ("zs", 0, 2), ("zs", 3, 0), ("zs", 0, 3), ("tx", 2, 0), ("yk", 3), ("tx", 2, 1),),
    (("zs", 0, 4), ("zs", 1, 1), ("zs", 2, 1),),
    (("zs", 1, 2), ("zs", 2, 2),),
    (("zs", 1, 3), ("zs", 2, 3), ("tx", 3, 0), ("zs", 1, 4), ("zs", 2, 4), ("tx", 3, 1),),
    (("zs", 3, 1), ("zs", 3, 2),),
    (("zs", 3, 3), ("zs", 3, 4),),
)
TAPS = (2, 0, 1, 3, 4)
HOSTS = (0, 1, 3)
PIECES = ((0, 2), (2, 2), (4, 1))
GROUPS = ((0, 1), (1, 1), (2, 1), (3, 1), (4, 1))


def step_kernel(
    dims,
    act, kern, cot,
    pooled_t, igrad, kgrad,
    weights, actv, cotv, slope, pairs32, g2x, dx,
    part, send1, recv1, send2, recv2, acc, send3, recv3,
    ahalo, dhalo, spread, psum, spans, kernv, lend,
    own_sem, a_sem, c_sem, ah_s, ah_r, dh_s, dh_r,
    az_s, az_r, ay_s, ay_r, ax_s, ax_r, ac_s, ac_r,
    r1_s, r1_r, r2_s, r2_r, r3_s, r3_r,
):
    n, A, taps, rows, T2, cin, cout = dims
    step = DILATION_STEP // 2
    mid = (taps - 1) // 2
    g = lax.axis_index("groups")
    p = lax.axis_index("pos")
    c = p % 2
    y = (p // 2) % 2
    z = p // 4
    high, low = z // 2, z % 2
    inner = jnp.logical_and(z > 0, z < A - 1)

    def copy(src, dst, ssem, rsem, to):
        return pltpu.make_async_remote_copy(
            src_ref=src, dst_ref=dst, send_sem=ssem, recv_sem=rsem, device_id=to, device_id_type=MESH
        )

    def at(zz, yy, cc):
        return (g, zz * 4 + yy * 2 + cc)

    core_peer, y_peer, x_peer = at(z, y, 1 - c), at(z, 1 - y, c), (1 - g, p)
    left, right = (g, (p + n - 1) % n), (g, (p + 1) % n)
    beside = (g, (p + n + 2 * c - 1) % n)

    order = (3 * (1 - high), 2 + high - 2 * low, 1 + low, z)
    near = (z, z + 1 - 2 * low, 2 - high, (A - 1) * (1 - high))
    onward = (None, A - 1 - z, near[1], near[1])

    own = pltpu.make_async_copy(kern, kernv, own_sem)
    acts = [
        pltpu.make_async_copy(act.at[:, pl.ds(j * LANES, LANES)], actv.at[j], a_sem.at[j])
        for j in range(A)
    ]
    cots = pltpu.make_async_copy(cot, cotv.at[pl.ds(0, cout)], c_sem)
    own.start()
    for one in acts:
        one.start()
    cots.start()

    wide = weights.shape[-1]
    whole = cout // LANES * LANES
    tail = cout - whole
    spare = wide - cout

    def lane_of(shape):
        return lax.broadcasted_iota(jnp.int32, shape, len(shape) - 1)

    def lent(host, donor, i):
        moved = pltpu.roll(donor, (tail - spare * i) % LANES, donor.ndim - 1)
        return jnp.where(lane_of(host.shape) < tail, host, moved)

    def returned(hosts):
        lane = lane_of(hosts[0].shape)
        found = jnp.zeros_like(hosts[0])
        for i, host in enumerate(hosts):
            moved = pltpu.roll(host, (spare * i - tail) % LANES, host.ndim - 1)
            inside = jnp.logical_and(lane >= spare * i, lane < spare * i + spare)
            found = jnp.where(inside, moved, found)
        return found

    barrier = pltpu.get_barrier_semaphore()
    for peer in (core_peer, beside, y_peer, x_peer, at(near[1], y, c)):
        pl.semaphore_signal(barrier, inc=1, device_id=peer, device_id_type=MESH)

    cotv[pl.ds(cout, spare), :] = jnp.zeros((spare, T2), BF16)
    own.wait()
    last = [
        jnp.concatenate(
            [
                kernv[t, :, :, pl.ds(whole, tail)].astype(F32).reshape(rows, tail),
                jnp.zeros((rows, spare), F32),
            ],
            axis=1,
        )
        for t in range(taps)
    ]
    for t in range(taps):
        held = lent(last[t], last[taps - 1], HOSTS.index(t)) if t in HOSTS else last[t]
        weights[t, z, y, c, :, :, pl.ds(0, whole)] = kernv[t, :, :, pl.ds(0, whole)]
        weights[t, z, y, c, :, :, pl.ds(whole, LANES)] = held.astype(BF16).reshape(
            2, rows // 2, LANES
        )

    @pl.when(inner)
    def _():
        pl.semaphore_signal(barrier, inc=1, device_id=at(near[2], y, c), device_id_type=MESH)
        pl.semaphore_wait(barrier, 6)

    @pl.when(jnp.logical_not(inner))
    def _():
        pl.semaphore_wait(barrier, 5)

    def column(j):
        return (y, 1 - y)[j]

    def share(zz, yy, half, q):
        first, count = PIECES[q]
        lanes = pl.ds(0, whole if first == taps - 1 else wide)
        return weights.at[pl.ds(first, count), zz, yy, c, half, :, lanes]

    def z_share(src, zz, j, slot, q, to):
        yy = column(j)
        return copy(
            src, share(zz, yy, g, q), az_s.at[slot, j, q], az_r.at[zz, yy, q], at(to, y, c)
        )

    def z_own(j, q, is_inner):
        src = share(z, column(j), g, q)
        sends = [z_share(src, z, j, 0, q, near[1])]
        if is_inner:
            sends.append(z_share(src, z, j, 4, q, near[2]))
        return sends

    def z_onward(i, j, q):
        zz = near[i]
        return z_share(share(zz, column(j), g, q), zz, j, i, q, onward[i])

    def y_share(q):
        block = share(z, y, g, q)
        return copy(block, block, ay_s.at[q], ay_r.at[q], y_peer)

    def x_share(zz, yy, q):
        block = share(zz, yy, g, q)
        return copy(block, block, ax_s.at[zz, yy, q], ax_r.at[zz, yy, q], x_peer)

    def core_block(zz, yy):
        block = weights.at[:, zz, yy, c]
        return copy(block, block, ac_s.at[zz, yy], ac_r.at[zz, yy], core_peer)

    def core_part(s, stage):
        if stage == 0:
            src, dst = send1.at[s, 1 - c, :, pl.ds(0, 1)], recv1.at[s, :, pl.ds(0, 1)]
        else:
            yy, rest = (1 - y, y)[stage - 1], pl.ds(1, taps - 1)
            src, dst = send1.at[s, 1 - c, yy, rest], recv1.at[s, yy, rest]
        return copy(src, dst, r1_s.at[s, stage], r1_r.at[s, stage], core_peer)

    def lanes_of(t):
        return pl.ds(0, whole if t == taps - 1 else wide)

    def group(ref, k):
        first, count = GROUPS[k]
        return ref.at[pl.ds(first, count), :, lanes_of(first)]

    def y_part(s, k):
        return copy(
            group(send2.at[s], k), group(recv2.at[s], k), r2_s.at[s, k], r2_r.at[s, k], y_peer
        )

    def z_part(s, k):
        up = (order[s] > z).astype(jnp.int32)
        return copy(
            group(send3.at[s], k), group(recv3.at[up, order[s]], k),
            r3_s.at[s, k], r3_r.at[up, order[s], k], at(z + 2 * up - 1, y, c),
        )

    def z_arrived(up, d, k):
        got = group(recv3.at[up, d], k)
        copy(got, got, r3_s.at[0, k], r3_r.at[up, d, k], y_peer).wait_recv()


    def ty(is_inner, q):
        y_share(q).wait_recv()
        return z_own(1, q, is_inner) + [x_share(z, 1 - y, q)]

    def tz(is_inner, i, j, q):
        zz, yy = near[i], column(j)
        got = share(zz, yy, g, q)
        copy(got, got, az_s.at[i, j, q], az_r.at[zz, yy, q], y_peer).wait_recv()
        return ([z_onward(i, j, q)] if is_inner else []) + [x_share(zz, yy, q)]

    def tx(is_inner, i, j):
        zz, yy = near[i], column(j)
        for q in range(len(PIECES)):
            got = share(zz, yy, 1 - g, q)
            copy(got, got, ax_s.at[zz, yy, q], ax_r.at[zz, yy, q], x_peer).wait_recv()
        return [core_block(zz, yy)]

    def y_sum(s, t):
        lanes = lanes_of(t)
        send2[s, t, :, lanes] = (
            part[s, t, 1 - y, c, :, lanes] + recv1[s, 1 - y, t, :, lanes].astype(F32)
        ).astype(BF16)

    def y_own(s, t):
        lanes = lanes_of(t)
        acc[s, t, :, lanes] = part[s, t, y, c, :, lanes] + recv1[s, y, t, :, lanes].astype(F32)

    def ym(is_inner, s):
        core_part(s, 0).wait_recv()
        y_sum(s, 0)
        y_part(s, 0).start()
        y_own(s, 0)
        return []

    def ys(is_inner, s):
        core_part(s, 1).wait_recv()
        for k in range(1, len(GROUPS)):
            for t in range(GROUPS[k][0], GROUPS[k][0] + GROUPS[k][1]):
                y_sum(s, t)
            y_part(s, k).start()
        return []

    def yk(is_inner, s):
        core_part(s, 2).wait_recv()
        for t in range(1, taps):
            y_own(s, t)
        return []

    def zs(is_inner, s, k):
        y_part(s, k).wait_recv()
        d = order[s]
        if s < A - 1:
            ups = [(d > z).astype(jnp.int32)] if is_inner else []
        else:
            ups = [0, 1] if is_inner else [(z > 0).astype(jnp.int32)]
        for up in ups:
            z_arrived(up, d, k)
        for t in range(GROUPS[k][0], GROUPS[k][0] + GROUPS[k][1]):
            lanes = lanes_of(t)
            total = acc[s, t, :, lanes] + recv2[s, t, :, lanes].astype(F32)
            for up in ups:
                total = total + recv3[up, d, t, :, lanes].astype(F32)
            if s < A - 1:
                send3[s, t, :, lanes] = total.astype(BF16)
            elif t < taps - 1:
                kgrad[TAPS[t]] = total[:, :cout]
                if TAPS[t] in HOSTS:
                    lend[HOSTS.index(TAPS[t])] = total[:, whole:]
            else:
                kgrad[TAPS[t], :, pl.ds(0, whole)] = total
                kgrad[TAPS[t], :, pl.ds(whole, tail)] = returned([lend[i] for i in range(3)])[
                    :, :tail
                ]
        return [z_part(s, k)] if s < A - 1 else []

    handlers = dict(ty=ty, tz=tz, tx=tx, ym=ym, ys=ys, yk=yk, zs=zs)

    def deal_with(i):
        def run(is_inner, events):
            for name, *index in events:
                for one in handlers[name](is_inner, *index):
                    one.start()

        if END[i]:
            pl.when(jnp.logical_not(inner))(lambda: run(False, END[i]))
        if INNER[i]:
            pl.when(inner)(lambda: run(True, INNER[i]))


    al = copy(act.at[pl.ds(0, 16)], ahalo.at[1], ah_s.at[0], ah_r.at[1], left)
    ar = copy(act.at[pl.ds(2 * T2 - 16, 16)], ahalo.at[0], ah_s.at[1], ah_r.at[0], right)
    dl = copy(dx.at[pl.ds(EDGE, 16)], dhalo.at[1], dh_s.at[0], dh_r.at[1], left)
    dr = copy(dx.at[pl.ds(EDGE + T2 - 16, 16)], dhalo.at[0], dh_s.at[1], dh_r.at[0], right)
    keep_left = (p > 0).astype(F32)
    keep_right = (p < n - 1).astype(F32)
    tile = pairs32.shape[0]

    def begin():
        def first(is_inner):
            for q in range(len(PIECES)):
                y_share(q).start()
                for one in z_own(0, q, is_inner):
                    one.start()
                if q == 0:
                    al.start()
                    ar.start()

        pl.when(inner)(lambda: first(True))
        pl.when(jnp.logical_not(inner))(lambda: first(False))
        core_block(z, y).start()

    def gelu_of(v):
        e = 0.5 * (1.0 + lax.erf(v * 0.7071067811865476))
        return (v * e).astype(BF16).astype(F32)

    def halved(count):
        return 0.5 * (
            pairs32[pl.ds(0, count, stride=2), :] + pairs32[pl.ds(1, count, stride=2), :]
        )

    def gelu():
        def body(i, carry):
            d = i // (2 * T2 // tile)
            r = i % (2 * T2 // tile)
            at_row = pl.multiple_of(r * tile, tile)
            pairs32[...] = gelu_of(actv[d, pl.ds(at_row, tile), :].astype(F32))
            half = pl.multiple_of(r * (tile // 2), tile // 2)
            g2x[d, pl.ds(PAD + half, tile // 2), :] = halved(tile // 2)
            return carry

        for one in acts:
            one.wait()
        lax.fori_loop(0, A * (2 * T2 // tile), body, 0)

    def cotangent():
        cots.wait()
        for i in range(T2 // LANES):
            dx[pl.ds(EDGE + i * LANES, LANES), :] = cotv[:, pl.ds(i * LANES, LANES)].T
        dl.start()
        dr.start()

    def slopes(d):
        def body(i, carry):
            at_row = pl.multiple_of(i * tile, tile)
            v = actv[d, pl.ds(at_row, tile), :].astype(F32)
            e = 0.25 * (1.0 + lax.erf(v * 0.7071067811865476))
            slope[d, pl.ds(at_row, tile), :] = e + v * jnp.exp(-0.5 * v * v) * 0.19947114020071635
            return carry

        lax.fori_loop(0, 2 * T2 // tile, body, 0)

    def halo():
        al.wait_recv()
        ar.wait_recv()
        for side, keep, at_row in ((0, keep_left, 0), (1, keep_right, PAD + T2)):
            for j in range(A):
                pairs32[pl.ds(0, 16), :] = gelu_of(
                    ahalo[side, :, pl.ds(j * LANES, LANES)].astype(F32)
                )
                g2x[j, pl.ds(at_row, PAD), :] = halved(PAD) * keep

    def turned(d, t):
        return g2x[d, pl.ds(PAD + step * (t - mid), T2), :].astype(BF16).T

    def times_cotangent(left_side):
        return jnp.dot(left_side, dx[pl.ds(EDGE, T2), :], preferred_element_type=F32)

    def keep(s, t, term):
        term = term.reshape(2, 2, rows, wide)
        part[s, t] = term
        for cc in range(2):
            for yy in range(2):
                send1[s, cc, yy, t] = term[yy, cc].astype(BF16)

    def dm():
        for s in range(A):
            keep(s, 0, times_cotangent(turned(order[s], mid)))
        for s in range(A):
            core_part(s, 0).start()

    def dot(b):
        both = range(2 * b, 2 * b + 2)
        for s in both:
            term = times_cotangent(
                jnp.concatenate([turned(order[s], t) for t in TAPS[1:]], axis=0)
            )
            terms = [term[i * LANES : i * LANES + LANES] for i in range(taps - 1)]
            for i, one in enumerate(terms):
                if TAPS[1 + i] in HOSTS:
                    lender = lent(
                        one[:, whole:], terms[-1][:, whole:], HOSTS.index(TAPS[1 + i])
                    )
                    one = jnp.concatenate([one[:, :whole], lender], axis=1)
                keep(s, 1 + i, one)
        for s in both:
            core_part(s, 1).start()
        for s in both:
            core_part(s, 2).start()

    def conv_weights(i):
        zz = near[i]
        some = weights[pl.ds(0, taps - 1), zz].reshape((taps - 1) * LANES, wide)
        tails = [
            weights[t, zz, :, :, :, :, pl.ds(whole, LANES)].reshape(LANES, LANES).astype(F32)
            for t in HOSTS
        ]
        donor = weights[taps - 1, zz, :, :, :, :, pl.ds(0, whole)].reshape(LANES, whole)
        donor = jnp.concatenate([donor, returned(tails).astype(BF16)], axis=1)
        return jnp.concatenate([some, donor], axis=0)

    def conv_wait(i):
        zz = near[i]
        for j in range(2):
            got = weights.at[:, zz, column(j), 1 - c]
            copy(
                got, got, ac_s.at[zz, column(j)], ac_r.at[zz, column(j)], core_peer
            ).wait_recv()
        if i == 0:
            dl.wait_recv()
            dr.wait_recv()
            dx[pl.ds(0, EDGE), :] = (dhalo[0].astype(F32) * keep_left).astype(BF16)
            dx[pl.ds(EDGE + T2, EDGE), :] = (dhalo[1].astype(F32) * keep_right).astype(BF16)

    def forward(i):
        window = jnp.concatenate(
            [
                g2x[near[i], pl.ds(PAD + step * (k - mid), T2), :].astype(BF16)
                for k in range(taps)
            ],
            axis=1,
        )
        total = jnp.dot(window, conv_weights(i), preferred_element_type=F32)
        if i > 0:
            total += psum[...]
        if i < A - 1:
            psum[...] = total
        else:
            done = total.astype(BF16)
            for q in range(T2 // LANES):
                pooled_t[:, pl.ds(q * LANES, LANES)] = done[q * LANES : q * LANES + LANES].T[:cout]

    def backward(i):
        spans[...] = lax.dot_general(
            dx[...], conv_weights(i), (((1,), (1,)), ((), ())), preferred_element_type=F32
        )
        grad = spans[pl.ds(EDGE + step * mid, T2), pl.ds(0, LANES)]
        for k in range(1, taps):
            grad += spans[pl.ds(EDGE - step * (k - mid), T2), pl.ds(k * LANES, LANES)]
        spread[pl.ds(0, T2, stride=2), :] = grad
        spread[pl.ds(1, T2, stride=2), :] = grad
        at_lane = pl.multiple_of(near[i] * LANES, LANES)
        igrad[:, pl.ds(at_lane, LANES)] = (spread[...] * slope[near[i]]).astype(BF16)

    def cf(i):
        conv_wait(i)
        forward(i)

    def cv(i):
        conv_wait(i)
        backward(i)
        forward(i)

    work = dict(
        start=begin, gelu=gelu, cot=cotangent, slope=slopes, halo=halo, dm=dm, dot=dot, cf=cf, cb=backward, cv=cv
    )
    for i, (name, *index) in enumerate(WORK):
        deal_with(i)
        work[name](*index)
    deal_with(len(WORK))


    for one in (al, ar, dl, dr):
        one.wait_send()

    def all_sent(is_inner):
        for q in range(len(PIECES)):
            for j in range(2):
                for one in z_own(j, q, is_inner):
                    one.wait_send()
                if is_inner:
                    for i in range(1, A):
                        z_onward(i, j, q).wait_send()

    pl.when(inner)(lambda: all_sent(True))
    pl.when(jnp.logical_not(inner))(lambda: all_sent(False))
    core_block(z, y).wait_send()
    for q in range(len(PIECES)):
        y_share(q).wait_send()
    for i in range(A):
        for j in range(2):
            if i or j:
                for q in range(len(PIECES)):
                    x_share(near[i], column(j), q).wait_send()
                core_block(near[i], column(j)).wait_send()
    for s in range(A):
        for stage in range(3):
            core_part(s, stage).wait_send()
        for k in range(len(GROUPS)):
            y_part(s, k).wait_send()
            if s < A - 1:
                z_part(s, k).wait_send()


def write_out(*refs):
    count = len(refs) // 2
    sems = refs[-1]
    copies = [
        pltpu.make_async_copy(refs[i], refs[count + i], sems.at[i]) for i in range(count)
    ]
    for one in copies:
        one.start()
    for one in copies:
        one.wait()


def on_device_fused(activations, kernel, cotangent):
    n = lax.axis_size("pos")
    A = n // 4
    rows, taps, cout = kernel.shape
    T2 = cotangent.shape[0]
    cin = activations.shape[1]
    dims = (n, A, taps, rows, T2, cin, cout)
    wide = -(-cout // LANES) * LANES
    Q, K = len(PIECES), len(GROUPS)
    kern = jnp.transpose(kernel, (1, 0, 2)).reshape(taps, 2, rows // 2, cout)
    vmem = pl.BlockSpec(memory_space=pltpu.VMEM)
    hbm = pl.BlockSpec(memory_space=pltpu.HBM)
    DMA = pltpu.SemaphoreType.DMA
    shapes = (
        jax.ShapeDtypeStruct((cout, T2), BF16),
        jax.ShapeDtypeStruct((2 * T2, cin), BF16),
        jax.ShapeDtypeStruct((taps, rows, cout), F32),
    )
    held = [
        pltpu.with_memory_space_constraint(one, pltpu.HBM)
        for one in (activations, kern, cotangent.T)
    ]
    results = pl.pallas_call(
        functools.partial(step_kernel, dims),
        out_shape=shapes,
        in_specs=[hbm] * 3,
        out_specs=(vmem,) * 3,
        scratch_shapes=[
            pltpu.VMEM((taps, A, 2, 2, 2, rows // 2, wide), BF16),
            pltpu.VMEM((A, 2 * T2, LANES), BF16),
            pltpu.VMEM((wide, T2), BF16),
            pltpu.VMEM((A, 2 * T2, LANES), F32),
            pltpu.VMEM((256, LANES), F32),
            pltpu.VMEM((A, T2 + 2 * PAD, LANES), F32),
            pltpu.VMEM((T2 + 2 * EDGE, wide), BF16),
            pltpu.VMEM((A, taps, 2, 2, rows, wide), F32),
            pltpu.VMEM((A, 2, 2, taps, rows, wide), BF16),
            pltpu.VMEM((A, 2, taps, rows, wide), BF16),
            pltpu.VMEM((A, taps, rows, wide), BF16),
            pltpu.VMEM((A, taps, rows, wide), BF16),
            pltpu.VMEM((A, taps, rows, wide), F32),
            pltpu.VMEM((A - 1, taps, rows, wide), BF16),
            pltpu.VMEM((2, A, taps, rows, wide), BF16),
            pltpu.VMEM((2, 16, cin), BF16),
            pltpu.VMEM((2, 16, wide), BF16),
            pltpu.VMEM((2 * T2, LANES), F32),
            pltpu.VMEM((T2, wide), F32),
            pltpu.VMEM((T2 + 2 * EDGE, taps * LANES), F32),
            pltpu.VMEM((taps, 2, rows // 2, cout), BF16),
            pltpu.VMEM((3, rows, LANES), F32),
            DMA, DMA((A,)), DMA, DMA((2,)), DMA((2,)), DMA((2,)), DMA((2,)),
            DMA((A + 1, 2, Q)), DMA((A, 2, Q)), DMA((Q,)), DMA((Q,)),
            DMA((A, 2, Q)), DMA((A, 2, Q)), DMA((A, 2)), DMA((A, 2)),
            DMA((A, 3)), DMA((A, 3)), DMA((A, K)), DMA((A, K)),
            DMA((A, K)), DMA((2, A, K)),
        ],
        compiler_params=pltpu.CompilerParams(
            collective_id=0, has_side_effects=True, vmem_limit_bytes=48 << 20
        ),
    )(*held)
    pooled_t, igrad, kgrad = pl.pallas_call(
        write_out,
        out_shape=shapes,
        in_specs=[vmem] * 3,
        out_specs=(hbm,) * 3,
        scratch_shapes=[DMA((3,))],
        compiler_params=pltpu.CompilerParams(has_side_effects=True, vmem_limit_bytes=1 << 20),
    )(*results)
    return pooled_t.T, igrad, jnp.transpose(kgrad, (1, 0, 2))


def solution(mesh):
    placed = (P(("groups", "pos"), None), P("pos", None, None), P(("groups", "pos"), None))
    n = mesh.shape["pos"]
    fused = n == 16 and mesh.shape["groups"] == 2
    return jax.shard_map(
        on_device_fused if fused else on_device,
        mesh=mesh,
        in_specs=placed,
        out_specs=(
            P(("groups", "pos"), None),
            P(("groups", "pos"), None),
            P(("groups", "pos"), None, None),
        ),
        check_vma=False,
    )
```

```python
import functools

import jax
import jax.numpy as jnp
from jax import lax
from jax.experimental import pallas as pl
from jax.experimental.pallas import tpu as pltpu
from jax.sharding import PartitionSpec as P

DILATION_STEP = 4


def extended(cells, sides, width):
    for axis, dim in sides:
        count = lax.axis_size(axis)
        ends = count - 1
        head = lax.slice_in_dim(cells, 0, width, axis=dim)
        tail = lax.slice_in_dim(cells, cells.shape[dim] - width, cells.shape[dim], axis=dim)
        cells = jnp.concatenate(
            [
                lax.ppermute(tail, axis, [(i, (i + 1) % count) for i in range(ends)]),
                cells,
                lax.ppermute(head, axis, [((i + 1) % count, i) for i in range(ends)]),
            ],
            axis=dim,
        )
    return cells


def gelu_value(v):
    return 0.5 * v * (1.0 + jax.scipy.special.erf(v * 0.7071067811865476))


def gelu_slope(v):
    return (
        0.5 * (1.0 + jax.scipy.special.erf(v * 0.7071067811865476))
        + v * jnp.exp(-0.5 * v * v) * 0.3989422804014327
    )


def on_device(activations, kernel, cotangent):
    window_length = activations.shape[0]
    kernel_taps = kernel.shape[1]
    out_width = kernel.shape[2]
    reach_row_count = (kernel_taps - 1) // 2 * DILATION_STEP
    values = activations.astype(jnp.float32)
    gelu = gelu_value(values).astype(jnp.bfloat16)
    padded_activation = extended(gelu, (("pos", 0),), reach_row_count)
    gelu_taps = jnp.stack(
        [
            padded_activation[
                tap_offset * DILATION_STEP : tap_offset * DILATION_STEP + window_length
            ]
            for tap_offset in range(kernel_taps)
        ]
    )
    kernel_full = lax.all_gather(kernel, "pos", axis=0, tiled=True)
    columns = gelu_taps
    dilated_output = jnp.einsum(
        "kpc,cko->po", columns, kernel_full, preferred_element_type=jnp.float32
    )
    pooled = (0.5 * dilated_output.reshape(window_length // 2, 2, out_width).sum(axis=1)).astype(
        jnp.bfloat16
    )
    convolution_gradient = (0.5 * jnp.repeat(cotangent.astype(jnp.float32), 2, axis=0)).astype(
        jnp.bfloat16
    )
    columns = gelu_taps
    kernel_grad = lax.psum_scatter(
        jnp.einsum(
            "kpc,po->cko", columns, convolution_gradient, preferred_element_type=jnp.float32
        ),
        "pos",
        scatter_dimension=0,
        tiled=True,
    )
    padded_gradient = extended(convolution_gradient, (("pos", 0),), reach_row_count)
    grad_taps = jnp.stack(
        [
            padded_gradient[
                (kernel_taps - 1 - tap_offset)
                * DILATION_STEP : (kernel_taps - 1 - tap_offset)
                * DILATION_STEP
                + window_length
            ]
            for tap_offset in range(kernel_taps)
        ]
    )
    block = jnp.einsum("kpo,cko->pc", grad_taps, kernel_full, preferred_element_type=jnp.float32)
    input_grad = (block * gelu_slope(values)).astype(jnp.bfloat16)
    return (pooled, input_grad, kernel_grad)


MESH = pl.DeviceIdType.MESH
F32 = jnp.float32
BF16 = jnp.bfloat16
PAD = 8
EDGE = 16
LANES = 128

WORK = (
    ("start",),
    ("gelu",),
    ("cot",),
    ("dm",),
    ("slope", 0),
    ("slope", 1),
    ("slope", 2),
    ("slope", 3),
    ("halo",),
    ("dot", 0),
    ("dot", 1),
    ("cf", 0),
    ("cb", 0),
    ("cf", 1),
    ("cb", 1),
    ("cf", 2),
    ("cb", 2),
    ("cv", 3),
)
END = (
    (),
    (),
    (),
    (),
    (),
    (),
    (),
    (),
    (("ty", 0), ("ym", 0), ("tz", 1, 0, 0), ("ym", 1),),
    (),
    (("ty", 1), ("ym", 2), ("ty", 2), ("ym", 3), ("tz", 1, 0, 1),),
    (("ys", 0), ("tz", 1, 0, 2), ("zs", 0, 0), ("tz", 1, 1, 0), ("yk", 0), ("ys", 1), ("tz", 2, 0, 0), ("zs", 1, 0), ("ys", 2), ("zs", 2, 0), ("yk", 1), ("tx", 0, 1), ("tz", 1, 1, 1), ("tz", 1, 1, 2), ("yk", 3), ("yk", 2), ("tz", 2, 0, 1), ("zs", 0, 1), ("tx", 1, 0),),
    (("zs", 0, 2), ("tz", 2, 0, 2), ("tz", 2, 1, 0), ("zs", 0, 3), ("tz", 2, 1, 1),),
    (("zs", 0, 4), ("tx", 1, 1), ("tz", 2, 1, 2), ("zs", 1, 1), ("tz", 3, 0, 0), ("tx", 2, 0), ("ys", 3), ("tz", 3, 0, 1), ("tz", 3, 0, 2), ("zs", 1, 2),),
    (("tz", 3, 1, 0), ("zs", 1, 3), ("tx", 2, 1), ("zs", 1, 4), ("tz", 3, 1, 1), ("tz", 3, 1, 2),),
    (("zs", 2, 1), ("zs", 2, 2),),
    (("tx", 3, 0), ("zs", 2, 3), ("zs", 3, 0),),
    (("tx", 3, 1), ("zs", 2, 4), ("zs", 3, 1), ("zs", 3, 2),),
    (("zs", 3, 3), ("zs", 3, 4),),
)
INNER = (
    (),
    (),
    (),
    (),
    (),
    (),
    (),
    (("ym", 0), ("ym", 1), ("ty", 0),),
    (("tz", 2, 0, 0), ("ym", 2), ("tz", 1, 0, 0), ("ym", 3),),
    (),
    (("ty", 1), ("ty", 2), ("tz", 1, 0, 1), ("tz", 2, 0, 1),),
    (("ys", 0), ("tz", 1, 0, 2), ("tz", 2, 0, 2), ("tz", 2, 1, 0), ("tz", 1, 1, 0), ("tz", 1, 1, 1), ("tz", 1, 1, 2), ("tz", 2, 1, 1), ("ys", 1), ("tx", 0, 1), ("yk", 2), ("tz", 2, 1, 2), ("tz", 3, 0, 0), ("ys", 2), ("zs", 0, 0), ("tz", 3, 0, 1), ("tz", 3, 0, 2), ("yk", 0), ("ys", 3),),
    (("tz", 3, 1, 0), ("zs", 2, 0), ("tz", 3, 1, 1), ("tx", 1, 0), ("tz", 3, 1, 2),),
    (("zs", 0, 1), ("yk", 1), ("zs", 1, 0), ("tx", 1, 1), ("zs", 0, 2), ("zs", 3, 0), ("zs", 0, 3), ("tx", 2, 0), ("yk", 3), ("tx", 2, 1),),
    (("zs", 0, 4), ("zs", 1, 1), ("zs", 2, 1),),
    (("zs", 1, 2), ("zs", 2, 2),),
    (("zs", 1, 3), ("zs", 2, 3), ("tx", 3, 0), ("zs", 1, 4), ("zs", 2, 4), ("tx", 3, 1),),
    (("zs", 3, 1), ("zs", 3, 2),),
    (("zs", 3, 3), ("zs", 3, 4),),
)
TAPS = (2, 0, 1, 3, 4)
HOSTS = (0, 1, 3)
PIECES = ((0, 2), (2, 2), (4, 1))
GROUPS = ((0, 1), (1, 1), (2, 1), (3, 1), (4, 1))


def step_kernel(
    dims,
    act, kern, cot,
    pooled_t, igrad, kgrad,
    weights, actv, cotv, slope, pairs32, g2x, dx,
    part, send1, recv1, send2, recv2, acc, send3, recv3,
    ahalo, dhalo, spread, psum, spans, kernv, lend,
    own_sem, a_sem, c_sem, ah_s, ah_r, dh_s, dh_r,
    az_s, az_r, ay_s, ay_r, ax_s, ax_r, ac_s, ac_r, al_s, al_r,
    r1_s, r1_r, r2_s, r2_r, r3_s, r3_r,
):
    n, A, taps, rows, T2, cin, cout = dims
    step = DILATION_STEP // 2
    mid = (taps - 1) // 2
    g = lax.axis_index("groups")
    p = lax.axis_index("pos")
    c = p % 2
    y = (p // 2) % 2
    z = p // 4
    high, low = z // 2, z % 2
    inner = jnp.logical_and(z > 0, z < A - 1)

    def copy(src, dst, ssem, rsem, to):
        return pltpu.make_async_remote_copy(
            src_ref=src, dst_ref=dst, send_sem=ssem, recv_sem=rsem, device_id=to, device_id_type=MESH
        )

    def at(zz, yy, cc):
        return (g, zz * 4 + yy * 2 + cc)

    core_peer, y_peer, x_peer = at(z, y, 1 - c), at(z, 1 - y, c), (1 - g, p)
    left, right = (g, (p + n - 1) % n), (g, (p + 1) % n)
    beside = (g, (p + n + 2 * c - 1) % n)

    order = (3 * (1 - high), 2 + high - 2 * low, 1 + low, z)
    near = (z, z + 1 - 2 * low, 2 - high, (A - 1) * (1 - high))
    onward = (None, A - 1 - z, near[1], near[1])

    own = pltpu.make_async_copy(kern, kernv, own_sem)
    acts = [
        pltpu.make_async_copy(act.at[:, pl.ds(j * LANES, LANES)], actv.at[j], a_sem.at[j])
        for j in range(A)
    ]
    cots = pltpu.make_async_copy(cot, cotv.at[pl.ds(0, cout)], c_sem)
    own.start()
    for one in acts:
        one.start()
    cots.start()

    wide = weights.shape[-1]
    whole = cout // LANES * LANES
    tail = cout - whole
    spare = wide - cout

    def lane_of(shape):
        return lax.broadcasted_iota(jnp.int32, shape, len(shape) - 1)

    def lent(host, donor, i):
        moved = pltpu.roll(donor, (tail - spare * i) % LANES, donor.ndim - 1)
        return jnp.where(lane_of(host.shape) < tail, host, moved)

    def returned(hosts):
        lane = lane_of(hosts[0].shape)
        found = jnp.zeros_like(hosts[0])
        for i, host in enumerate(hosts):
            moved = pltpu.roll(host, (spare * i - tail) % LANES, host.ndim - 1)
            inside = jnp.logical_and(lane >= spare * i, lane < spare * i + spare)
            found = jnp.where(inside, moved, found)
        return found

    barrier = pltpu.get_barrier_semaphore()
    for peer in (core_peer, beside, y_peer, x_peer, at(near[1], y, c)):
        pl.semaphore_signal(barrier, inc=1, device_id=peer, device_id_type=MESH)

    cotv[pl.ds(cout, spare), :] = jnp.zeros((spare, T2), BF16)
    own.wait()
    last = [
        jnp.concatenate(
            [
                kernv[t, :, :, pl.ds(whole, tail)].astype(F32).reshape(rows, tail),
                jnp.zeros((rows, spare), F32),
            ],
            axis=1,
        )
        for t in range(taps)
    ]
    for t in range(taps):
        held = lent(last[t], last[taps - 1], HOSTS.index(t)) if t in HOSTS else last[t]
        weights[t, z, y, c, :, :, pl.ds(0, whole)] = kernv[t, :, :, pl.ds(0, whole)]
        weights[t, z, y, c, :, :, pl.ds(whole, LANES)] = held.astype(BF16).reshape(
            2, rows // 2, LANES
        )

    @pl.when(inner)
    def _():
        pl.semaphore_signal(barrier, inc=1, device_id=at(near[2], y, c), device_id_type=MESH)
        pl.semaphore_wait(barrier, 6)

    @pl.when(jnp.logical_not(inner))
    def _():
        pl.semaphore_wait(barrier, 5)

    def column(j):
        return (y, 1 - y)[j]

    def share(zz, yy, half, q):
        first, count = PIECES[q]
        lanes = pl.ds(0, whole if first == taps - 1 else wide)
        return weights.at[pl.ds(first, count), zz, yy, c, half, :, lanes]

    def z_share(src, zz, j, slot, q, to):
        yy = column(j)
        return copy(
            src, share(zz, yy, g, q), az_s.at[slot, j, q], az_r.at[zz, yy, q], at(to, y, c)
        )

    def z_own(j, q, is_inner):
        src = share(z, column(j), g, q)
        sends = [z_share(src, z, j, 0, q, near[1])]
        if is_inner:
            sends.append(z_share(src, z, j, 4, q, near[2]))
        return sends

    def z_onward(i, j, q):
        zz = near[i]
        return z_share(share(zz, column(j), g, q), zz, j, i, q, onward[i])

    def y_share(q):
        block = share(z, y, g, q)
        return copy(block, block, ay_s.at[q], ay_r.at[q], y_peer)

    def x_share(zz, yy, q):
        block = share(zz, yy, g, q)
        return copy(block, block, ax_s.at[zz, yy, q], ax_r.at[zz, yy, q], x_peer)

    def core_block(zz, yy):
        block = weights.at[:, zz, yy, c]
        return copy(block, block, ac_s.at[zz, yy], ac_r.at[zz, yy], core_peer)

    def core_piece(yy, q):
        first, count = PIECES[q]
        block = weights.at[pl.ds(first, count), near[A - 1], yy, c]
        return copy(block, block, al_s.at[yy, q], al_r.at[yy, q], core_peer)

    def core_part(s, stage):
        if stage == 0:
            src, dst = send1.at[s, 1 - c, :, pl.ds(0, 1)], recv1.at[s, :, pl.ds(0, 1)]
        else:
            yy, rest = (1 - y, y)[stage - 1], pl.ds(1, taps - 1)
            src, dst = send1.at[s, 1 - c, yy, rest], recv1.at[s, yy, rest]
        return copy(src, dst, r1_s.at[s, stage], r1_r.at[s, stage], core_peer)

    def lanes_of(t):
        return pl.ds(0, whole if t == taps - 1 else wide)

    def group(ref, k):
        first, count = GROUPS[k]
        return ref.at[pl.ds(first, count), :, lanes_of(first)]

    def y_part(s, k):
        return copy(
            group(send2.at[s], k), group(recv2.at[s], k), r2_s.at[s, k], r2_r.at[s, k], y_peer
        )

    def z_part(s, k):
        up = (order[s] > z).astype(jnp.int32)
        return copy(
            group(send3.at[s], k), group(recv3.at[up, order[s]], k),
            r3_s.at[s, k], r3_r.at[up, order[s], k], at(z + 2 * up - 1, y, c),
        )

    def z_arrived(up, d, k):
        got = group(recv3.at[up, d], k)
        copy(got, got, r3_s.at[0, k], r3_r.at[up, d, k], y_peer).wait_recv()


    def ty(is_inner, q):
        y_share(q).wait_recv()
        return z_own(1, q, is_inner) + [x_share(z, 1 - y, q)]

    def tz(is_inner, i, j, q):
        zz, yy = near[i], column(j)
        got = share(zz, yy, g, q)
        copy(got, got, az_s.at[i, j, q], az_r.at[zz, yy, q], y_peer).wait_recv()
        return ([z_onward(i, j, q)] if is_inner else []) + [x_share(zz, yy, q)]

    def tx(is_inner, i, j):
        zz, yy = near[i], column(j)
        for q in range(len(PIECES)):
            got = share(zz, yy, 1 - g, q)
            copy(got, got, ax_s.at[zz, yy, q], ax_r.at[zz, yy, q], x_peer).wait_recv()
            if i == A - 1:
                core_piece(yy, q).start()
        return [core_block(zz, yy)] if i < A - 1 else []

    def y_sum(s, t):
        lanes = lanes_of(t)
        send2[s, t, :, lanes] = (
            part[s, t, 1 - y, c, :, lanes] + recv1[s, 1 - y, t, :, lanes].astype(F32)
        ).astype(BF16)

    def y_own(s, t):
        lanes = lanes_of(t)
        acc[s, t, :, lanes] = part[s, t, y, c, :, lanes] + recv1[s, y, t, :, lanes].astype(F32)

    def ym(is_inner, s):
        core_part(s, 0).wait_recv()
        y_sum(s, 0)
        y_part(s, 0).start()
        y_own(s, 0)
        return []

    def ys(is_inner, s):
        core_part(s, 1).wait_recv()
        for k in range(1, len(GROUPS)):
            for t in range(GROUPS[k][0], GROUPS[k][0] + GROUPS[k][1]):
                y_sum(s, t)
            y_part(s, k).start()
        return []

    def yk(is_inner, s):
        core_part(s, 2).wait_recv()
        for t in range(1, taps):
            y_own(s, t)
        return []

    def zs(is_inner, s, k):
        y_part(s, k).wait_recv()
        d = order[s]
        if s < A - 1:
            ups = [(d > z).astype(jnp.int32)] if is_inner else []
        else:
            ups = [0, 1] if is_inner else [(z > 0).astype(jnp.int32)]
        for up in ups:
            z_arrived(up, d, k)
        for t in range(GROUPS[k][0], GROUPS[k][0] + GROUPS[k][1]):
            lanes = lanes_of(t)
            total = acc[s, t, :, lanes] + recv2[s, t, :, lanes].astype(F32)
            for up in ups:
                total = total + recv3[up, d, t, :, lanes].astype(F32)
            if s < A - 1:
                send3[s, t, :, lanes] = total.astype(BF16)
            elif t < taps - 1:
                kgrad[TAPS[t]] = total[:, :cout]
                if TAPS[t] in HOSTS:
                    lend[HOSTS.index(TAPS[t])] = total[:, whole:]
            else:
                kgrad[TAPS[t], :, pl.ds(0, whole)] = total
                kgrad[TAPS[t], :, pl.ds(whole, tail)] = returned([lend[i] for i in range(3)])[
                    :, :tail
                ]
        return [z_part(s, k)] if s < A - 1 else []

    handlers = dict(ty=ty, tz=tz, tx=tx, ym=ym, ys=ys, yk=yk, zs=zs)

    def deal_with(i):
        def run(is_inner, events):
            for name, *index in events:
                for one in handlers[name](is_inner, *index):
                    one.start()

        if END[i]:
            pl.when(jnp.logical_not(inner))(lambda: run(False, END[i]))
        if INNER[i]:
            pl.when(inner)(lambda: run(True, INNER[i]))


    al = copy(act.at[pl.ds(0, 16)], ahalo.at[1], ah_s.at[0], ah_r.at[1], left)
    ar = copy(act.at[pl.ds(2 * T2 - 16, 16)], ahalo.at[0], ah_s.at[1], ah_r.at[0], right)
    dl = copy(dx.at[pl.ds(EDGE, 16)], dhalo.at[1], dh_s.at[0], dh_r.at[1], left)
    dr = copy(dx.at[pl.ds(EDGE + T2 - 16, 16)], dhalo.at[0], dh_s.at[1], dh_r.at[0], right)
    keep_left = (p > 0).astype(F32)
    keep_right = (p < n - 1).astype(F32)
    tile = pairs32.shape[0]

    def begin():
        def first(is_inner):
            for q in range(len(PIECES)):
                y_share(q).start()
                for one in z_own(0, q, is_inner):
                    one.start()
                if q == 0:
                    al.start()
                    ar.start()

        pl.when(inner)(lambda: first(True))
        pl.when(jnp.logical_not(inner))(lambda: first(False))
        core_block(z, y).start()

    def gelu_of(v):
        e = 0.5 * (1.0 + lax.erf(v * 0.7071067811865476))
        return (v * e).astype(BF16).astype(F32)

    def halved(count):
        return 0.5 * (
            pairs32[pl.ds(0, count, stride=2), :] + pairs32[pl.ds(1, count, stride=2), :]
        )

    def gelu():
        def body(i, carry):
            d = i // (2 * T2 // tile)
            r = i % (2 * T2 // tile)
            at_row = pl.multiple_of(r * tile, tile)
            pairs32[...] = gelu_of(actv[d, pl.ds(at_row, tile), :].astype(F32))
            half = pl.multiple_of(r * (tile // 2), tile // 2)
            g2x[d, pl.ds(PAD + half, tile // 2), :] = halved(tile // 2)
            return carry

        for one in acts:
            one.wait()
        lax.fori_loop(0, A * (2 * T2 // tile), body, 0)

    def cotangent():
        cots.wait()
        for i in range(T2 // LANES):
            dx[pl.ds(EDGE + i * LANES, LANES), :] = cotv[:, pl.ds(i * LANES, LANES)].T
        dl.start()
        dr.start()

    def slopes(d):
        def body(i, carry):
            at_row = pl.multiple_of(i * tile, tile)
            v = actv[d, pl.ds(at_row, tile), :].astype(F32)
            e = 0.25 * (1.0 + lax.erf(v * 0.7071067811865476))
            slope[d, pl.ds(at_row, tile), :] = e + v * jnp.exp(-0.5 * v * v) * 0.19947114020071635
            return carry

        lax.fori_loop(0, 2 * T2 // tile, body, 0)

    def halo():
        al.wait_recv()
        ar.wait_recv()
        for side, keep, at_row in ((0, keep_left, 0), (1, keep_right, PAD + T2)):
            for j in range(A):
                pairs32[pl.ds(0, 16), :] = gelu_of(
                    ahalo[side, :, pl.ds(j * LANES, LANES)].astype(F32)
                )
                g2x[j, pl.ds(at_row, PAD), :] = halved(PAD) * keep

    def turned(d, t):
        return g2x[d, pl.ds(PAD + step * (t - mid), T2), :].astype(BF16).T

    def times_cotangent(left_side):
        return jnp.dot(left_side, dx[pl.ds(EDGE, T2), :], preferred_element_type=F32)

    def keep(s, t, term):
        term = term.reshape(2, 2, rows, wide)
        part[s, t] = term
        for cc in range(2):
            for yy in range(2):
                send1[s, cc, yy, t] = term[yy, cc].astype(BF16)

    def dm():
        for s in range(A):
            keep(s, 0, times_cotangent(turned(order[s], mid)))
        for s in range(A):
            core_part(s, 0).start()

    def dot(b):
        both = range(2 * b, 2 * b + 2)
        for s in both:
            term = times_cotangent(
                jnp.concatenate([turned(order[s], t) for t in TAPS[1:]], axis=0)
            )
            terms = [term[i * LANES : i * LANES + LANES] for i in range(taps - 1)]
            for i, one in enumerate(terms):
                if TAPS[1 + i] in HOSTS:
                    lender = lent(
                        one[:, whole:], terms[-1][:, whole:], HOSTS.index(TAPS[1 + i])
                    )
                    one = jnp.concatenate([one[:, :whole], lender], axis=1)
                keep(s, 1 + i, one)
        for s in both:
            core_part(s, 1).start()
        for s in both:
            core_part(s, 2).start()

    def conv_weights(i):
        zz = near[i]
        some = weights[pl.ds(0, taps - 1), zz].reshape((taps - 1) * LANES, wide)
        tails = [
            weights[t, zz, :, :, :, :, pl.ds(whole, LANES)].reshape(LANES, LANES).astype(F32)
            for t in HOSTS
        ]
        donor = weights[taps - 1, zz, :, :, :, :, pl.ds(0, whole)].reshape(LANES, whole)
        donor = jnp.concatenate([donor, returned(tails).astype(BF16)], axis=1)
        return jnp.concatenate([some, donor], axis=0)

    def conv_wait(i):
        zz = near[i]
        for j in range(2):
            if i == A - 1:
                for q, (first, count) in enumerate(PIECES):
                    got = weights.at[pl.ds(first, count), zz, column(j), 1 - c]
                    copy(
                        got, got, al_s.at[column(j), q], al_r.at[column(j), q], core_peer
                    ).wait_recv()
                continue
            got = weights.at[:, zz, column(j), 1 - c]
            copy(
                got, got, ac_s.at[zz, column(j)], ac_r.at[zz, column(j)], core_peer
            ).wait_recv()
        if i == 0:
            dl.wait_recv()
            dr.wait_recv()
            dx[pl.ds(0, EDGE), :] = (dhalo[0].astype(F32) * keep_left).astype(BF16)
            dx[pl.ds(EDGE + T2, EDGE), :] = (dhalo[1].astype(F32) * keep_right).astype(BF16)

    def forward(i):
        window = jnp.concatenate(
            [
                g2x[near[i], pl.ds(PAD + step * (k - mid), T2), :].astype(BF16)
                for k in range(taps)
            ],
            axis=1,
        )
        total = jnp.dot(window, conv_weights(i), preferred_element_type=F32)
        if i > 0:
            total += psum[...]
        if i < A - 1:
            psum[...] = total
        else:
            done = total.astype(BF16)
            for q in range(T2 // LANES):
                pooled_t[:, pl.ds(q * LANES, LANES)] = done[q * LANES : q * LANES + LANES].T[:cout]

    def backward(i):
        spans[...] = lax.dot_general(
            dx[...], conv_weights(i), (((1,), (1,)), ((), ())), preferred_element_type=F32
        )
        grad = spans[pl.ds(EDGE + step * mid, T2), pl.ds(0, LANES)]
        for k in range(1, taps):
            grad += spans[pl.ds(EDGE - step * (k - mid), T2), pl.ds(k * LANES, LANES)]
        spread[pl.ds(0, T2, stride=2), :] = grad
        spread[pl.ds(1, T2, stride=2), :] = grad
        at_lane = pl.multiple_of(near[i] * LANES, LANES)
        igrad[:, pl.ds(at_lane, LANES)] = (spread[...] * slope[near[i]]).astype(BF16)

    def cf(i):
        conv_wait(i)
        forward(i)

    def cv(i):
        conv_wait(i)
        backward(i)
        forward(i)

    work = dict(
        start=begin, gelu=gelu, cot=cotangent, slope=slopes, halo=halo, dm=dm, dot=dot, cf=cf, cb=backward, cv=cv
    )
    for i, (name, *index) in enumerate(WORK):
        deal_with(i)
        work[name](*index)
    deal_with(len(WORK))


    for one in (al, ar, dl, dr):
        one.wait_send()

    def all_sent(is_inner):
        for q in range(len(PIECES)):
            for j in range(2):
                for one in z_own(j, q, is_inner):
                    one.wait_send()
                if is_inner:
                    for i in range(1, A):
                        z_onward(i, j, q).wait_send()

    pl.when(inner)(lambda: all_sent(True))
    pl.when(jnp.logical_not(inner))(lambda: all_sent(False))
    core_block(z, y).wait_send()
    for q in range(len(PIECES)):
        y_share(q).wait_send()
    for i in range(A):
        for j in range(2):
            if i or j:
                for q in range(len(PIECES)):
                    x_share(near[i], column(j), q).wait_send()
                    if i == A - 1:
                        core_piece(column(j), q).wait_send()
                if i < A - 1:
                    core_block(near[i], column(j)).wait_send()
    for s in range(A):
        for stage in range(3):
            core_part(s, stage).wait_send()
        for k in range(len(GROUPS)):
            y_part(s, k).wait_send()
            if s < A - 1:
                z_part(s, k).wait_send()


def write_out(*refs):
    count = len(refs) // 2
    sems = refs[-1]
    copies = [
        pltpu.make_async_copy(refs[i], refs[count + i], sems.at[i]) for i in range(count)
    ]
    for one in copies:
        one.start()
    for one in copies:
        one.wait()


def on_device_fused(activations, kernel, cotangent):
    n = lax.axis_size("pos")
    A = n // 4
    rows, taps, cout = kernel.shape
    T2 = cotangent.shape[0]
    cin = activations.shape[1]
    dims = (n, A, taps, rows, T2, cin, cout)
    wide = -(-cout // LANES) * LANES
    Q, K = len(PIECES), len(GROUPS)
    kern = jnp.transpose(kernel, (1, 0, 2)).reshape(taps, 2, rows // 2, cout)
    vmem = pl.BlockSpec(memory_space=pltpu.VMEM)
    hbm = pl.BlockSpec(memory_space=pltpu.HBM)
    DMA = pltpu.SemaphoreType.DMA
    shapes = (
        jax.ShapeDtypeStruct((cout, T2), BF16),
        jax.ShapeDtypeStruct((2 * T2, cin), BF16),
        jax.ShapeDtypeStruct((taps, rows, cout), F32),
    )
    held = [
        pltpu.with_memory_space_constraint(one, pltpu.HBM)
        for one in (activations, kern, cotangent.T)
    ]
    results = pl.pallas_call(
        functools.partial(step_kernel, dims),
        out_shape=shapes,
        in_specs=[hbm] * 3,
        out_specs=(vmem,) * 3,
        scratch_shapes=[
            pltpu.VMEM((taps, A, 2, 2, 2, rows // 2, wide), BF16),
            pltpu.VMEM((A, 2 * T2, LANES), BF16),
            pltpu.VMEM((wide, T2), BF16),
            pltpu.VMEM((A, 2 * T2, LANES), F32),
            pltpu.VMEM((256, LANES), F32),
            pltpu.VMEM((A, T2 + 2 * PAD, LANES), F32),
            pltpu.VMEM((T2 + 2 * EDGE, wide), BF16),
            pltpu.VMEM((A, taps, 2, 2, rows, wide), F32),
            pltpu.VMEM((A, 2, 2, taps, rows, wide), BF16),
            pltpu.VMEM((A, 2, taps, rows, wide), BF16),
            pltpu.VMEM((A, taps, rows, wide), BF16),
            pltpu.VMEM((A, taps, rows, wide), BF16),
            pltpu.VMEM((A, taps, rows, wide), F32),
            pltpu.VMEM((A - 1, taps, rows, wide), BF16),
            pltpu.VMEM((2, A, taps, rows, wide), BF16),
            pltpu.VMEM((2, 16, cin), BF16),
            pltpu.VMEM((2, 16, wide), BF16),
            pltpu.VMEM((2 * T2, LANES), F32),
            pltpu.VMEM((T2, wide), F32),
            pltpu.VMEM((T2 + 2 * EDGE, taps * LANES), F32),
            pltpu.VMEM((taps, 2, rows // 2, cout), BF16),
            pltpu.VMEM((3, rows, LANES), F32),
            DMA, DMA((A,)), DMA, DMA((2,)), DMA((2,)), DMA((2,)), DMA((2,)),
            DMA((A + 1, 2, Q)), DMA((A, 2, Q)), DMA((Q,)), DMA((Q,)),
            DMA((A, 2, Q)), DMA((A, 2, Q)), DMA((A, 2)), DMA((A, 2)), DMA((2, Q)), DMA((2, Q)),
            DMA((A, 3)), DMA((A, 3)), DMA((A, K)), DMA((A, K)),
            DMA((A, K)), DMA((2, A, K)),
        ],
        compiler_params=pltpu.CompilerParams(
            collective_id=0, has_side_effects=True, vmem_limit_bytes=48 << 20
        ),
    )(*held)
    pooled_t, igrad, kgrad = pl.pallas_call(
        write_out,
        out_shape=shapes,
        in_specs=[vmem] * 3,
        out_specs=(hbm,) * 3,
        scratch_shapes=[DMA((3,))],
        compiler_params=pltpu.CompilerParams(has_side_effects=True, vmem_limit_bytes=1 << 20),
    )(*results)
    return pooled_t.T, igrad, jnp.transpose(kgrad, (1, 0, 2))


def solution(mesh):
    placed = (P(("groups", "pos"), None), P("pos", None, None), P(("groups", "pos"), None))
    n = mesh.shape["pos"]
    fused = n == 16 and mesh.shape["groups"] == 2
    return jax.shard_map(
        on_device_fused if fused else on_device,
        mesh=mesh,
        in_specs=placed,
        out_specs=(
            P(("groups", "pos"), None),
            P(("groups", "pos"), None),
            P(("groups", "pos"), None, None),
        ),
        check_vma=False,
    )
```

```python
import functools

import jax
import jax.numpy as jnp
from jax import lax
from jax.experimental import pallas as pl
from jax.experimental.pallas import tpu as pltpu
from jax.sharding import PartitionSpec as P

DILATION_STEP = 4


def extended(cells, sides, width):
    for axis, dim in sides:
        count = lax.axis_size(axis)
        ends = count - 1
        head = lax.slice_in_dim(cells, 0, width, axis=dim)
        tail = lax.slice_in_dim(cells, cells.shape[dim] - width, cells.shape[dim], axis=dim)
        cells = jnp.concatenate(
            [
                lax.ppermute(tail, axis, [(i, (i + 1) % count) for i in range(ends)]),
                cells,
                lax.ppermute(head, axis, [((i + 1) % count, i) for i in range(ends)]),
            ],
            axis=dim,
        )
    return cells


def gelu_value(v):
    return 0.5 * v * (1.0 + jax.scipy.special.erf(v * 0.7071067811865476))


def gelu_slope(v):
    return (
        0.5 * (1.0 + jax.scipy.special.erf(v * 0.7071067811865476))
        + v * jnp.exp(-0.5 * v * v) * 0.3989422804014327
    )


def on_device(activations, kernel, cotangent):
    window_length = activations.shape[0]
    kernel_taps = kernel.shape[1]
    out_width = kernel.shape[2]
    reach_row_count = (kernel_taps - 1) // 2 * DILATION_STEP
    values = activations.astype(jnp.float32)
    gelu = gelu_value(values).astype(jnp.bfloat16)
    padded_activation = extended(gelu, (("pos", 0),), reach_row_count)
    gelu_taps = jnp.stack(
        [
            padded_activation[
                tap_offset * DILATION_STEP : tap_offset * DILATION_STEP + window_length
            ]
            for tap_offset in range(kernel_taps)
        ]
    )
    kernel_full = lax.all_gather(kernel, "pos", axis=0, tiled=True)
    columns = gelu_taps
    dilated_output = jnp.einsum(
        "kpc,cko->po", columns, kernel_full, preferred_element_type=jnp.float32
    )
    pooled = (0.5 * dilated_output.reshape(window_length // 2, 2, out_width).sum(axis=1)).astype(
        jnp.bfloat16
    )
    convolution_gradient = (0.5 * jnp.repeat(cotangent.astype(jnp.float32), 2, axis=0)).astype(
        jnp.bfloat16
    )
    columns = gelu_taps
    kernel_grad = lax.psum_scatter(
        jnp.einsum(
            "kpc,po->cko", columns, convolution_gradient, preferred_element_type=jnp.float32
        ),
        "pos",
        scatter_dimension=0,
        tiled=True,
    )
    padded_gradient = extended(convolution_gradient, (("pos", 0),), reach_row_count)
    grad_taps = jnp.stack(
        [
            padded_gradient[
                (kernel_taps - 1 - tap_offset)
                * DILATION_STEP : (kernel_taps - 1 - tap_offset)
                * DILATION_STEP
                + window_length
            ]
            for tap_offset in range(kernel_taps)
        ]
    )
    block = jnp.einsum("kpo,cko->pc", grad_taps, kernel_full, preferred_element_type=jnp.float32)
    input_grad = (block * gelu_slope(values)).astype(jnp.bfloat16)
    return (pooled, input_grad, kernel_grad)


MESH = pl.DeviceIdType.MESH
F32 = jnp.float32
BF16 = jnp.bfloat16
PAD = 8
EDGE = 16
LANES = 128

WORK = (
    ("start",),
    ("gelu",),
    ("cot",),
    ("dm",),
    ("slope", 0),
    ("slope", 1),
    ("slope", 2),
    ("slope", 3),
    ("halo",),
    ("dot", 0),
    ("dot", 1),
    ("cf", 0),
    ("cb", 0),
    ("cf", 1),
    ("cb", 1),
    ("cf", 2),
    ("cb", 2),
    ("cv", 3),
)
END = (
    (),
    (),
    (),
    (),
    (),
    (),
    (),
    (),
    (("ty", 0), ("ym", 0), ("tz", 1, 0, 0), ("ym", 1),),
    (),
    (("ty", 1), ("ym", 2), ("ty", 2), ("ym", 3), ("tz", 1, 0, 1),),
    (("ys", 0), ("tz", 1, 0, 2), ("zs", 0, 0), ("tz", 1, 1, 0), ("yk", 0), ("ys", 1), ("tz", 2, 0, 0), ("zs", 1, 0), ("ys", 2), ("zs", 2, 0), ("yk", 1), ("tx", 0, 1), ("tz", 1, 1, 1), ("tz", 1, 1, 2), ("yk", 3), ("yk", 2), ("tz", 2, 0, 1), ("zs", 0, 1), ("tx", 1, 0),),
    (("zs", 0, 2), ("tz", 2, 0, 2), ("tz", 2, 1, 0), ("zs", 0, 3), ("tz", 2, 1, 1),),
    (("zs", 0, 4), ("tx", 1, 1), ("tz", 2, 1, 2), ("zs", 1, 1), ("tz", 3, 0, 0), ("tx", 2, 0), ("ys", 3), ("tz", 3, 0, 1), ("tz", 3, 0, 2), ("zs", 1, 2),),
    (("tz", 3, 1, 0), ("zs", 1, 3), ("tx", 2, 1), ("zs", 1, 4), ("tz", 3, 1, 1), ("tz", 3, 1, 2),),
    (("zs", 2, 1), ("zs", 2, 2),),
    (("tx", 3, 0), ("zs", 2, 3), ("zs", 3, 0),),
    (("tx", 3, 1), ("zs", 2, 4), ("zs", 3, 1), ("zs", 3, 2),),
    (("zs", 3, 3), ("zs", 3, 4),),
)
INNER = (
    (),
    (),
    (),
    (),
    (),
    (),
    (),
    (("ym", 0), ("ym", 1), ("ty", 0),),
    (("tz", 2, 0, 0), ("ym", 2), ("tz", 1, 0, 0), ("ym", 3),),
    (),
    (("ty", 1), ("ty", 2), ("tz", 1, 0, 1), ("tz", 2, 0, 1),),
    (("ys", 0), ("tz", 1, 0, 2), ("tz", 2, 0, 2), ("tz", 2, 1, 0), ("tz", 1, 1, 0), ("tz", 1, 1, 1), ("tz", 1, 1, 2), ("tz", 2, 1, 1), ("ys", 1), ("tx", 0, 1), ("yk", 2), ("tz", 2, 1, 2), ("tz", 3, 0, 0), ("ys", 2), ("zs", 0, 0), ("tz", 3, 0, 1), ("tz", 3, 0, 2), ("yk", 0), ("ys", 3),),
    (("tz", 3, 1, 0), ("zs", 2, 0), ("tz", 3, 1, 1), ("tx", 1, 0), ("tz", 3, 1, 2),),
    (("zs", 0, 1), ("yk", 1), ("zs", 1, 0), ("tx", 1, 1), ("zs", 0, 2), ("zs", 3, 0), ("zs", 0, 3), ("tx", 2, 0), ("yk", 3), ("tx", 2, 1),),
    (("zs", 0, 4), ("zs", 1, 1), ("zs", 2, 1),),
    (("zs", 1, 2), ("zs", 2, 2),),
    (("zs", 1, 3), ("zs", 2, 3), ("tx", 3, 0), ("zs", 1, 4), ("zs", 2, 4), ("tx", 3, 1),),
    (("zs", 3, 1), ("zs", 3, 2),),
    (("zs", 3, 3), ("zs", 3, 4),),
)
TAPS = (2, 0, 1, 3, 4)
HOSTS = (0, 1, 3)
PIECES = ((0, 2), (2, 2), (4, 1))
GROUPS = ((0, 1), (1, 1), (2, 1), (3, 1), (4, 1))


def step_kernel(
    dims,
    act, kern, cot,
    pooled_t, igrad, kgrad,
    weights, actv, cotv, slope, pairs32, g2x, dx,
    part, send1, recv1, send2, recv2, acc, send3, recv3,
    ahalo, dedge, dhalo, spread, psum, spans, kernv, lend,
    own_sem, a_sem, c_sem, ah_s, ah_r, dh_s, dh_r,
    az_s, az_r, ay_s, ay_r, ax_s, ax_r, ac_s, ac_r, al_s, al_r,
    r1_s, r1_r, r2_s, r2_r, r3_s, r3_r,
):
    n, A, taps, rows, T2, cin, cout = dims
    step = DILATION_STEP // 2
    mid = (taps - 1) // 2
    g = lax.axis_index("groups")
    p = lax.axis_index("pos")
    c = p % 2
    y = (p // 2) % 2
    z = p // 4
    high, low = z // 2, z % 2
    inner = jnp.logical_and(z > 0, z < A - 1)

    def copy(src, dst, ssem, rsem, to):
        return pltpu.make_async_remote_copy(
            src_ref=src, dst_ref=dst, send_sem=ssem, recv_sem=rsem, device_id=to, device_id_type=MESH
        )

    def at(zz, yy, cc):
        return (g, zz * 4 + yy * 2 + cc)

    core_peer, y_peer, x_peer = at(z, y, 1 - c), at(z, 1 - y, c), (1 - g, p)
    left, right = (g, (p + n - 1) % n), (g, (p + 1) % n)
    beside = (g, (p + n + 2 * c - 1) % n)

    order = (3 * (1 - high), 2 + high - 2 * low, 1 + low, z)
    near = (z, z + 1 - 2 * low, 2 - high, (A - 1) * (1 - high))
    onward = (None, A - 1 - z, near[1], near[1])

    own = pltpu.make_async_copy(kern, kernv, own_sem)
    acts = [
        pltpu.make_async_copy(act.at[:, pl.ds(j * LANES, LANES)], actv.at[j], a_sem.at[j])
        for j in range(A)
    ]
    cots = pltpu.make_async_copy(cot, cotv.at[pl.ds(0, cout)], c_sem)
    own.start()
    for one in acts:
        one.start()
    cots.start()

    wide = weights.shape[-1]
    whole = cout // LANES * LANES
    tail = cout - whole
    spare = wide - cout

    def lane_of(shape):
        return lax.broadcasted_iota(jnp.int32, shape, len(shape) - 1)

    def lent(host, donor, i):
        moved = pltpu.roll(donor, (tail - spare * i) % LANES, donor.ndim - 1)
        return jnp.where(lane_of(host.shape) < tail, host, moved)

    def returned(hosts):
        lane = lane_of(hosts[0].shape)
        found = jnp.zeros_like(hosts[0])
        for i, host in enumerate(hosts):
            moved = pltpu.roll(host, (spare * i - tail) % LANES, host.ndim - 1)
            inside = jnp.logical_and(lane >= spare * i, lane < spare * i + spare)
            found = jnp.where(inside, moved, found)
        return found

    barrier = pltpu.get_barrier_semaphore()
    for peer in (core_peer, beside, y_peer, x_peer, at(near[1], y, c)):
        pl.semaphore_signal(barrier, inc=1, device_id=peer, device_id_type=MESH)

    cotv[pl.ds(cout, spare), :] = jnp.zeros((spare, T2), BF16)
    own.wait()
    last = [
        jnp.concatenate(
            [
                kernv[t, :, :, pl.ds(whole, tail)].astype(F32).reshape(rows, tail),
                jnp.zeros((rows, spare), F32),
            ],
            axis=1,
        )
        for t in range(taps)
    ]
    for t in range(taps):
        held = lent(last[t], last[taps - 1], HOSTS.index(t)) if t in HOSTS else last[t]
        weights[t, z, y, c, :, :, pl.ds(0, whole)] = kernv[t, :, :, pl.ds(0, whole)]
        weights[t, z, y, c, :, :, pl.ds(whole, LANES)] = held.astype(BF16).reshape(
            2, rows // 2, LANES
        )

    @pl.when(inner)
    def _():
        pl.semaphore_signal(barrier, inc=1, device_id=at(near[2], y, c), device_id_type=MESH)
        pl.semaphore_wait(barrier, 6)

    @pl.when(jnp.logical_not(inner))
    def _():
        pl.semaphore_wait(barrier, 5)

    def column(j):
        return (y, 1 - y)[j]

    def share(zz, yy, half, q):
        first, count = PIECES[q]
        lanes = pl.ds(0, whole if first == taps - 1 else wide)
        return weights.at[pl.ds(first, count), zz, yy, c, half, :, lanes]

    def z_share(src, zz, j, slot, q, to):
        yy = column(j)
        return copy(
            src, share(zz, yy, g, q), az_s.at[slot, j, q], az_r.at[zz, yy, q], at(to, y, c)
        )

    def z_own(j, q, is_inner):
        src = share(z, column(j), g, q)
        sends = [z_share(src, z, j, 0, q, near[1])]
        if is_inner:
            sends.append(z_share(src, z, j, 4, q, near[2]))
        return sends

    def z_onward(i, j, q):
        zz = near[i]
        return z_share(share(zz, column(j), g, q), zz, j, i, q, onward[i])

    def y_share(q):
        block = share(z, y, g, q)
        return copy(block, block, ay_s.at[q], ay_r.at[q], y_peer)

    def x_share(zz, yy, q):
        block = share(zz, yy, g, q)
        return copy(block, block, ax_s.at[zz, yy, q], ax_r.at[zz, yy, q], x_peer)

    def core_block(zz, yy):
        block = weights.at[:, zz, yy, c]
        return copy(block, block, ac_s.at[zz, yy], ac_r.at[zz, yy], core_peer)

    def core_piece(yy, q):
        first, count = PIECES[q]
        block = weights.at[pl.ds(first, count), near[A - 1], yy, c]
        return copy(block, block, al_s.at[yy, q], al_r.at[yy, q], core_peer)

    def core_part(s, stage):
        if stage == 0:
            src, dst = send1.at[s, 1 - c, :, pl.ds(0, 1)], recv1.at[s, :, pl.ds(0, 1)]
        else:
            yy, rest = (1 - y, y)[stage - 1], pl.ds(1, taps - 1)
            src, dst = send1.at[s, 1 - c, yy, rest], recv1.at[s, yy, rest]
        return copy(src, dst, r1_s.at[s, stage], r1_r.at[s, stage], core_peer)

    def lanes_of(t):
        return pl.ds(0, whole if t == taps - 1 else wide)

    def group(ref, k):
        first, count = GROUPS[k]
        return ref.at[pl.ds(first, count), :, lanes_of(first)]

    def y_part(s, k):
        return copy(
            group(send2.at[s], k), group(recv2.at[s], k), r2_s.at[s, k], r2_r.at[s, k], y_peer
        )

    def z_part(s, k):
        up = (order[s] > z).astype(jnp.int32)
        return copy(
            group(send3.at[s], k), group(recv3.at[up, order[s]], k),
            r3_s.at[s, k], r3_r.at[up, order[s], k], at(z + 2 * up - 1, y, c),
        )

    def z_arrived(up, d, k):
        got = group(recv3.at[up, d], k)
        copy(got, got, r3_s.at[0, k], r3_r.at[up, d, k], y_peer).wait_recv()


    def ty(is_inner, q):
        y_share(q).wait_recv()
        return z_own(1, q, is_inner) + [x_share(z, 1 - y, q)]

    def tz(is_inner, i, j, q):
        zz, yy = near[i], column(j)
        got = share(zz, yy, g, q)
        copy(got, got, az_s.at[i, j, q], az_r.at[zz, yy, q], y_peer).wait_recv()
        return ([z_onward(i, j, q)] if is_inner else []) + [x_share(zz, yy, q)]

    def tx(is_inner, i, j):
        zz, yy = near[i], column(j)
        for q in range(len(PIECES)):
            got = share(zz, yy, 1 - g, q)
            copy(got, got, ax_s.at[zz, yy, q], ax_r.at[zz, yy, q], x_peer).wait_recv()
            if i == A - 1:
                core_piece(yy, q).start()
        return [core_block(zz, yy)] if i < A - 1 else []

    def y_sum(s, t):
        lanes = lanes_of(t)
        send2[s, t, :, lanes] = (
            part[s, t, 1 - y, c, :, lanes] + recv1[s, 1 - y, t, :, lanes].astype(F32)
        ).astype(BF16)

    def y_own(s, t):
        lanes = lanes_of(t)
        acc[s, t, :, lanes] = part[s, t, y, c, :, lanes] + recv1[s, y, t, :, lanes].astype(F32)

    def ym(is_inner, s):
        core_part(s, 0).wait_recv()
        y_sum(s, 0)
        y_part(s, 0).start()
        y_own(s, 0)
        return []

    def ys(is_inner, s):
        core_part(s, 1).wait_recv()
        for k in range(1, len(GROUPS)):
            for t in range(GROUPS[k][0], GROUPS[k][0] + GROUPS[k][1]):
                y_sum(s, t)
            y_part(s, k).start()
        return []

    def yk(is_inner, s):
        core_part(s, 2).wait_recv()
        for t in range(1, taps):
            y_own(s, t)
        return []

    def zs(is_inner, s, k):
        y_part(s, k).wait_recv()
        d = order[s]
        if s < A - 1:
            ups = [(d > z).astype(jnp.int32)] if is_inner else []
        else:
            ups = [0, 1] if is_inner else [(z > 0).astype(jnp.int32)]
        for up in ups:
            z_arrived(up, d, k)
        for t in range(GROUPS[k][0], GROUPS[k][0] + GROUPS[k][1]):
            lanes = lanes_of(t)
            total = acc[s, t, :, lanes] + recv2[s, t, :, lanes].astype(F32)
            for up in ups:
                total = total + recv3[up, d, t, :, lanes].astype(F32)
            if s < A - 1:
                send3[s, t, :, lanes] = total.astype(BF16)
            elif t < taps - 1:
                kgrad[TAPS[t]] = total[:, :cout]
                if TAPS[t] in HOSTS:
                    lend[HOSTS.index(TAPS[t])] = total[:, whole:]
            else:
                kgrad[TAPS[t], :, pl.ds(0, whole)] = total
                kgrad[TAPS[t], :, pl.ds(whole, tail)] = returned([lend[i] for i in range(3)])[
                    :, :tail
                ]
        return [z_part(s, k)] if s < A - 1 else []

    handlers = dict(ty=ty, tz=tz, tx=tx, ym=ym, ys=ys, yk=yk, zs=zs)

    def deal_with(i):
        def run(is_inner, events):
            for name, *index in events:
                for one in handlers[name](is_inner, *index):
                    one.start()

        if END[i]:
            pl.when(jnp.logical_not(inner))(lambda: run(False, END[i]))
        if INNER[i]:
            pl.when(inner)(lambda: run(True, INNER[i]))


    al = copy(act.at[pl.ds(0, 16)], ahalo.at[1], ah_s.at[0], ah_r.at[1], left)
    ar = copy(act.at[pl.ds(2 * T2 - 16, 16)], ahalo.at[0], ah_s.at[1], ah_r.at[0], right)
    dl = copy(dedge.at[0], dhalo.at[1], dh_s.at[0], dh_r.at[1], left)
    dr = copy(dedge.at[1], dhalo.at[0], dh_s.at[1], dh_r.at[0], right)
    keep_left = (p > 0).astype(F32)
    keep_right = (p < n - 1).astype(F32)
    tile = pairs32.shape[0]

    def begin():
        def first(is_inner):
            for q in range(len(PIECES)):
                y_share(q).start()
                for one in z_own(0, q, is_inner):
                    one.start()
                if q == 0:
                    al.start()
                    ar.start()

        pl.when(inner)(lambda: first(True))
        pl.when(jnp.logical_not(inner))(lambda: first(False))
        core_block(z, y).start()

    def gelu_of(v):
        e = 0.5 * (1.0 + lax.erf(v * 0.7071067811865476))
        return (v * e).astype(BF16).astype(F32)

    def halved(count):
        return 0.5 * (
            pairs32[pl.ds(0, count, stride=2), :] + pairs32[pl.ds(1, count, stride=2), :]
        )

    def gelu():
        def body(i, carry):
            d = i // (2 * T2 // tile)
            r = i % (2 * T2 // tile)
            at_row = pl.multiple_of(r * tile, tile)
            pairs32[...] = gelu_of(actv[d, pl.ds(at_row, tile), :].astype(F32))
            half = pl.multiple_of(r * (tile // 2), tile // 2)
            g2x[d, pl.ds(PAD + half, tile // 2), :] = halved(tile // 2)
            return carry

        for one in acts:
            one.wait()
        lax.fori_loop(0, A * (2 * T2 // tile), body, 0)

    reach = step * mid

    def folded(some):
        tiles = [some[:, j * LANES : j * LANES + LANES] for j in range(wide // LANES)]
        count = 16 // reach
        beside = tiles[count:] + [jnp.zeros_like(tiles[0])] * (2 * count - len(tiles))
        return jnp.concatenate(
            [jnp.concatenate(tiles[:count], axis=0), jnp.concatenate(beside, axis=0)], axis=1
        ).astype(BF16)

    def unfolded(held):
        held = held.astype(F32)
        count = 16 // reach
        return jnp.concatenate(
            [
                held[
                    j % count * reach : j % count * reach + reach,
                    j // count * LANES : j // count * LANES + LANES,
                ]
                for j in range(wide // LANES)
            ],
            axis=1,
        )

    def cotangent():
        cots.wait()
        for i in range(T2 // LANES):
            dx[pl.ds(EDGE + i * LANES, LANES), :] = cotv[:, pl.ds(i * LANES, LANES)].T
        dedge[0] = folded(dx[pl.ds(EDGE, 16), :].astype(F32)[:reach])
        dedge[1] = folded(dx[pl.ds(EDGE + T2 - 16, 16), :].astype(F32)[16 - reach :])
        dl.start()
        dr.start()

    def slopes(d):
        def body(i, carry):
            at_row = pl.multiple_of(i * tile, tile)
            v = actv[d, pl.ds(at_row, tile), :].astype(F32)
            e = 0.25 * (1.0 + lax.erf(v * 0.7071067811865476))
            slope[d, pl.ds(at_row, tile), :] = e + v * jnp.exp(-0.5 * v * v) * 0.19947114020071635
            return carry

        lax.fori_loop(0, 2 * T2 // tile, body, 0)

    def halo():
        al.wait_recv()
        ar.wait_recv()
        for side, keep, at_row in ((0, keep_left, 0), (1, keep_right, PAD + T2)):
            for j in range(A):
                pairs32[pl.ds(0, 16), :] = gelu_of(
                    ahalo[side, :, pl.ds(j * LANES, LANES)].astype(F32)
                )
                g2x[j, pl.ds(at_row, PAD), :] = halved(PAD) * keep

    def turned(d, t):
        return g2x[d, pl.ds(PAD + step * (t - mid), T2), :].astype(BF16).T

    def times_cotangent(left_side):
        return jnp.dot(left_side, dx[pl.ds(EDGE, T2), :], preferred_element_type=F32)

    def keep(s, t, term):
        term = term.reshape(2, 2, rows, wide)
        part[s, t] = term
        for cc in range(2):
            for yy in range(2):
                send1[s, cc, yy, t] = term[yy, cc].astype(BF16)

    def dm():
        for s in range(A):
            keep(s, 0, times_cotangent(turned(order[s], mid)))
        for s in range(A):
            core_part(s, 0).start()

    def dot(b):
        both = range(2 * b, 2 * b + 2)
        for s in both:
            term = times_cotangent(
                jnp.concatenate([turned(order[s], t) for t in TAPS[1:]], axis=0)
            )
            terms = [term[i * LANES : i * LANES + LANES] for i in range(taps - 1)]
            for i, one in enumerate(terms):
                if TAPS[1 + i] in HOSTS:
                    lender = lent(
                        one[:, whole:], terms[-1][:, whole:], HOSTS.index(TAPS[1 + i])
                    )
                    one = jnp.concatenate([one[:, :whole], lender], axis=1)
                keep(s, 1 + i, one)
        for s in both:
            core_part(s, 1).start()
        for s in both:
            core_part(s, 2).start()

    def conv_weights(i):
        zz = near[i]
        some = weights[pl.ds(0, taps - 1), zz].reshape((taps - 1) * LANES, wide)
        tails = [
            weights[t, zz, :, :, :, :, pl.ds(whole, LANES)].reshape(LANES, LANES).astype(F32)
            for t in HOSTS
        ]
        donor = weights[taps - 1, zz, :, :, :, :, pl.ds(0, whole)].reshape(LANES, whole)
        donor = jnp.concatenate([donor, returned(tails).astype(BF16)], axis=1)
        return jnp.concatenate([some, donor], axis=0)

    def conv_wait(i):
        zz = near[i]
        for j in range(2):
            if i == A - 1:
                for q, (first, count) in enumerate(PIECES):
                    got = weights.at[pl.ds(first, count), zz, column(j), 1 - c]
                    copy(
                        got, got, al_s.at[column(j), q], al_r.at[column(j), q], core_peer
                    ).wait_recv()
                continue
            got = weights.at[:, zz, column(j), 1 - c]
            copy(
                got, got, ac_s.at[zz, column(j)], ac_r.at[zz, column(j)], core_peer
            ).wait_recv()
        if i == 0:
            dl.wait_recv()
            dr.wait_recv()
            rest = jnp.zeros((EDGE - reach, wide), F32)
            before, after = unfolded(dhalo[0]) * keep_left, unfolded(dhalo[1]) * keep_right
            dx[pl.ds(0, EDGE), :] = jnp.concatenate([rest, before], axis=0).astype(BF16)
            dx[pl.ds(EDGE + T2, EDGE), :] = jnp.concatenate([after, rest], axis=0).astype(BF16)

    def forward(i):
        window = jnp.concatenate(
            [
                g2x[near[i], pl.ds(PAD + step * (k - mid), T2), :].astype(BF16)
                for k in range(taps)
            ],
            axis=1,
        )
        total = jnp.dot(window, conv_weights(i), preferred_element_type=F32)
        if i > 0:
            total += psum[...]
        if i < A - 1:
            psum[...] = total
        else:
            done = total.astype(BF16)
            for q in range(T2 // LANES):
                pooled_t[:, pl.ds(q * LANES, LANES)] = done[q * LANES : q * LANES + LANES].T[:cout]

    def backward(i):
        spans[...] = lax.dot_general(
            dx[...], conv_weights(i), (((1,), (1,)), ((), ())), preferred_element_type=F32
        )
        grad = spans[pl.ds(EDGE + step * mid, T2), pl.ds(0, LANES)]
        for k in range(1, taps):
            grad += spans[pl.ds(EDGE - step * (k - mid), T2), pl.ds(k * LANES, LANES)]
        spread[pl.ds(0, T2, stride=2), :] = grad
        spread[pl.ds(1, T2, stride=2), :] = grad
        at_lane = pl.multiple_of(near[i] * LANES, LANES)
        igrad[:, pl.ds(at_lane, LANES)] = (spread[...] * slope[near[i]]).astype(BF16)

    def cf(i):
        conv_wait(i)
        forward(i)

    def cv(i):
        conv_wait(i)
        backward(i)
        forward(i)

    work = dict(
        start=begin, gelu=gelu, cot=cotangent, slope=slopes, halo=halo, dm=dm, dot=dot, cf=cf, cb=backward, cv=cv
    )
    for i, (name, *index) in enumerate(WORK):
        deal_with(i)
        work[name](*index)
    deal_with(len(WORK))


    for one in (al, ar, dl, dr):
        one.wait_send()

    def all_sent(is_inner):
        for q in range(len(PIECES)):
            for j in range(2):
                for one in z_own(j, q, is_inner):
                    one.wait_send()
                if is_inner:
                    for i in range(1, A):
                        z_onward(i, j, q).wait_send()

    pl.when(inner)(lambda: all_sent(True))
    pl.when(jnp.logical_not(inner))(lambda: all_sent(False))
    core_block(z, y).wait_send()
    for q in range(len(PIECES)):
        y_share(q).wait_send()
    for i in range(A):
        for j in range(2):
            if i or j:
                for q in range(len(PIECES)):
                    x_share(near[i], column(j), q).wait_send()
                    if i == A - 1:
                        core_piece(column(j), q).wait_send()
                if i < A - 1:
                    core_block(near[i], column(j)).wait_send()
    for s in range(A):
        for stage in range(3):
            core_part(s, stage).wait_send()
        for k in range(len(GROUPS)):
            y_part(s, k).wait_send()
            if s < A - 1:
                z_part(s, k).wait_send()


def write_out(*refs):
    count = len(refs) // 2
    sems = refs[-1]
    copies = [
        pltpu.make_async_copy(refs[i], refs[count + i], sems.at[i]) for i in range(count)
    ]
    for one in copies:
        one.start()
    for one in copies:
        one.wait()


def on_device_fused(activations, kernel, cotangent):
    n = lax.axis_size("pos")
    A = n // 4
    rows, taps, cout = kernel.shape
    T2 = cotangent.shape[0]
    cin = activations.shape[1]
    dims = (n, A, taps, rows, T2, cin, cout)
    wide = -(-cout // LANES) * LANES
    Q, K = len(PIECES), len(GROUPS)
    kern = jnp.transpose(kernel, (1, 0, 2)).reshape(taps, 2, rows // 2, cout)
    vmem = pl.BlockSpec(memory_space=pltpu.VMEM)
    hbm = pl.BlockSpec(memory_space=pltpu.HBM)
    DMA = pltpu.SemaphoreType.DMA
    shapes = (
        jax.ShapeDtypeStruct((cout, T2), BF16),
        jax.ShapeDtypeStruct((2 * T2, cin), BF16),
        jax.ShapeDtypeStruct((taps, rows, cout), F32),
    )
    held = [
        pltpu.with_memory_space_constraint(one, pltpu.HBM)
        for one in (activations, kern, cotangent.T)
    ]
    results = pl.pallas_call(
        functools.partial(step_kernel, dims),
        out_shape=shapes,
        in_specs=[hbm] * 3,
        out_specs=(vmem,) * 3,
        scratch_shapes=[
            pltpu.VMEM((taps, A, 2, 2, 2, rows // 2, wide), BF16),
            pltpu.VMEM((A, 2 * T2, LANES), BF16),
            pltpu.VMEM((wide, T2), BF16),
            pltpu.VMEM((A, 2 * T2, LANES), F32),
            pltpu.VMEM((256, LANES), F32),
            pltpu.VMEM((A, T2 + 2 * PAD, LANES), F32),
            pltpu.VMEM((T2 + 2 * EDGE, wide), BF16),
            pltpu.VMEM((A, taps, 2, 2, rows, wide), F32),
            pltpu.VMEM((A, 2, 2, taps, rows, wide), BF16),
            pltpu.VMEM((A, 2, taps, rows, wide), BF16),
            pltpu.VMEM((A, taps, rows, wide), BF16),
            pltpu.VMEM((A, taps, rows, wide), BF16),
            pltpu.VMEM((A, taps, rows, wide), F32),
            pltpu.VMEM((A - 1, taps, rows, wide), BF16),
            pltpu.VMEM((2, A, taps, rows, wide), BF16),
            pltpu.VMEM((2, 16, cin), BF16),
            pltpu.VMEM((2, 16, 2 * LANES), BF16),
            pltpu.VMEM((2, 16, 2 * LANES), BF16),
            pltpu.VMEM((2 * T2, LANES), F32),
            pltpu.VMEM((T2, wide), F32),
            pltpu.VMEM((T2 + 2 * EDGE, taps * LANES), F32),
            pltpu.VMEM((taps, 2, rows // 2, cout), BF16),
            pltpu.VMEM((3, rows, LANES), F32),
            DMA, DMA((A,)), DMA, DMA((2,)), DMA((2,)), DMA((2,)), DMA((2,)),
            DMA((A + 1, 2, Q)), DMA((A, 2, Q)), DMA((Q,)), DMA((Q,)),
            DMA((A, 2, Q)), DMA((A, 2, Q)), DMA((A, 2)), DMA((A, 2)), DMA((2, Q)), DMA((2, Q)),
            DMA((A, 3)), DMA((A, 3)), DMA((A, K)), DMA((A, K)),
            DMA((A, K)), DMA((2, A, K)),
        ],
        compiler_params=pltpu.CompilerParams(
            collective_id=0, has_side_effects=True, vmem_limit_bytes=48 << 20
        ),
    )(*held)
    pooled_t, igrad, kgrad = pl.pallas_call(
        write_out,
        out_shape=shapes,
        in_specs=[vmem] * 3,
        out_specs=(hbm,) * 3,
        scratch_shapes=[DMA((3,))],
        compiler_params=pltpu.CompilerParams(has_side_effects=True, vmem_limit_bytes=1 << 20),
    )(*results)
    return pooled_t.T, igrad, jnp.transpose(kgrad, (1, 0, 2))


def solution(mesh):
    placed = (P(("groups", "pos"), None), P("pos", None, None), P(("groups", "pos"), None))
    n = mesh.shape["pos"]
    fused = n == 16 and mesh.shape["groups"] == 2
    return jax.shard_map(
        on_device_fused if fused else on_device,
        mesh=mesh,
        in_specs=placed,
        out_specs=(
            P(("groups", "pos"), None),
            P(("groups", "pos"), None),
            P(("groups", "pos"), None, None),
        ),
        check_vma=False,
    )
```
